512 devices in a mesh: seq: 32 (over z, core), heads: 4 (over x), dp: 4 (over y).
Axes of the slice: x: 4, y: 4, z: 16, core: 2. Of those that a mesh axis runs over, the one named last changes fastest.
Arguments:
- tokens: bfloat16 [4, 4096, 3072], P('dp', 'seq'), may hold values from -6 to 6
- proj_weights: bfloat16 [3, 3072, 4096], P(None, 'seq', ('heads', 'dp')), may hold values from -0.109375 to 0.109375
- norm_gain: float32 [4096], P(('heads', 'dp')), may hold values from 0.5 to 1.5
Outputs:
- attended: bfloat16 [4, 4096, 4096], P('dp', 'seq', 'heads')
The draws below stay inside these ranges and needn't reach their ends.
All inputs are finite; a program needn't handle non-finite values.
Results may differ from the reference program's by a relative error of at most 0.0063.
Values may be sent and summed in bfloat16 or wider, within the bound.
No kernel may reach another device: no remote copies, remote signals or barrier semaphores. Data moves between devices by JAX's collectives and lax.ppermute only.
A program may use at most 64 MiB of HBM per device.

```python
import jax
import jax.numpy as jnp
from jax import lax

D = 3072
HEADS = 32
DH = 128
TOK_DEV = 128
SEQS = 4
LENGTH = 4096
N_SEQ = 32


def level_of(rng, extent, shards, smallest, top_value):
    def one(dim, blocks):
        draws = jax.random.uniform(jax.random.fold_in(jax.random.fold_in(rng, 6), dim), (blocks,), jnp.float32, smallest / len(shards), top_value / len(shards))
        return jnp.repeat(jnp.exp(draws), extent[dim] // blocks).reshape((-1,) + (1,) * (len(extent) - dim - 1))

    level = one(*shards[0])
    for cut in shards[1:]:
        level = level * one(*cut)
    return level


def scatter_about(own_key, extent, width, limit, split=(), kind=jnp.bfloat16):
    drawn = jax.random.normal(own_key, extent, jnp.float32) * width
    if len(split) > 0:
        drawn = level_of(own_key, extent, split, -0.22, 0.18) * drawn
    return jnp.clip(drawn, min=-limit, max=limit).astype(kind)


def setup_inputs(seed: int = 0) -> dict:
    arg_keys = jax.random.split(jax.random.key(seed), 4)
    tokens = scatter_about(arg_keys[0], (SEQS, LENGTH, D), 1.0, 6.0, ((0, 4), (1, 32)))
    proj_weights = scatter_about(arg_keys[1], (3, D, HEADS * DH), D ** -0.5, 0.109375, ((1, 32), (2, 16)))
    norm_gain = jnp.clip(1.0 + 0.1 * jax.random.normal(arg_keys[2], (HEADS * DH,), jnp.float32), 0.5, 1.5)
    return {"tokens": tokens, "proj_weights": proj_weights, "norm_gain": norm_gain}


def one_sequence(rows, proj_weights, norm_gain):
    blocks = N_SEQ
    queries = jax.nn.silu(jnp.dot(rows, proj_weights[0], preferred_element_type=jnp.float32)).astype(jnp.bfloat16)
    keys = jax.nn.silu(jnp.dot(rows, proj_weights[1], preferred_element_type=jnp.float32)).astype(jnp.bfloat16)
    values = jnp.dot(rows, proj_weights[2], preferred_element_type=jnp.float32).astype(jnp.bfloat16)
    query_f = queries.astype(jnp.float32).reshape(blocks, TOK_DEV, HEADS, DH)
    key_f = keys.astype(jnp.float32).reshape(blocks, TOK_DEV, HEADS, DH)
    value_f = values.astype(jnp.float32).reshape(blocks, TOK_DEV, HEADS, DH)
    state = jnp.einsum('nthd,nthe->nhde', key_f, value_f)
    running = jnp.cumsum(state, axis=0)
    prefix = jnp.concatenate([jnp.zeros((1, HEADS, DH, DH), jnp.float32), running[:-1]], axis=0)
    prefix_b = prefix.astype(jnp.bfloat16).astype(jnp.float32)
    scores = jnp.einsum('nthd,nuhd->nhtu', query_f, key_f)
    causal = lax.broadcasted_iota(jnp.int32, (TOK_DEV, TOK_DEV), 0) >= lax.broadcasted_iota(jnp.int32, (TOK_DEV, TOK_DEV), 1)
    scores_b = jnp.where(causal, scores, 0.0).astype(jnp.bfloat16).astype(jnp.float32)
    local = jnp.einsum('nhtu,nuhd->nthd', scores_b, value_f)
    carried = jnp.einsum('nthd,nhde->nthe', query_f, prefix_b)
    attn = local + carried
    scale = lax.rsqrt(lax.optimization_barrier(jnp.mean(attn * attn, axis=-1, keepdims=True)) + 1e-06)
    normed = attn * scale * norm_gain.reshape(HEADS, DH)
    return normed.reshape(LENGTH, HEADS * DH).astype(jnp.bfloat16)

def reference(tokens, proj_weights, norm_gain):
    results = [one_sequence(tokens[index], proj_weights, norm_gain) for index in range(SEQS)]
    return jnp.stack(results, axis=0)
```

```python
import jax
import jax.numpy as jnp
from jax import lax
from jax.sharding import PartitionSpec as P

DH = 128
SEQ = 32
WSCALE = 2.0**19
SAME_CORE = [[2 * z + c for z in range(16)] for c in range(2)]
SIBLING = [(i, i ^ 1) for i in range(SEQ)]
QUAD = [[8 * a + 2 * b + c for b in range(4)] for a in range(4) for c in range(2)]
ACROSS = [[8 * a + 2 * b + c for a in range(4)] for b in range(4) for c in range(2)]
F32 = jnp.float32
B16 = jnp.bfloat16


def body(tokens, proj_weights, norm_gain):
    place = lax.axis_index("seq")
    core = place % 2
    quad_place = (place // 2) % 4
    quad = place // 8
    mine_t = lax.all_to_all(jnp.broadcast_to(tokens, (4,) + tokens.shape[1:]), "dp", 0, 0, tiled=True)
    wh = (proj_weights.astype(F32) * WSCALE).astype(jnp.float16)
    wh = jnp.transpose(wh, (1, 0, 2)).reshape(96, 3, 2, DH)
    head0, head1 = wh[:, :, 0].reshape(96, 3 * DH), wh[:, :, 1].reshape(96, 3 * DH)
    first = core == 0
    keep = jnp.where(first, head0, head1)
    give = jnp.where(first, head1, head0)
    got = lax.ppermute(give, "seq", SIBLING)
    rows = jnp.concatenate([jnp.where(first, keep, got), jnp.where(first, got, keep)], axis=0)
    full = lax.all_gather(rows, "seq", axis=0, tiled=True, axis_index_groups=SAME_CORE)
    mine_t, full = lax.optimization_barrier((mine_t, full))
    weights = (full.astype(F32) * (1.0 / WSCALE)).astype(B16)
    other_t = lax.ppermute(mine_t, "seq", SIBLING)

    def project(t):
        out = jnp.dot(t.reshape(4 * 128, -1), weights, preferred_element_type=F32)
        out = out.reshape(4, 128, 3, DH)
        return (jax.nn.silu(out[:, :, 0]).astype(B16), jax.nn.silu(out[:, :, 1]).astype(B16), out[:, :, 2].astype(B16))

    qa, ka, va = project(mine_t)
    qb, kb, vb = project(other_t)
    sa = jnp.einsum("std,ste->sde", ka, va, preferred_element_type=F32)
    sb = jnp.einsum("std,ste->sde", kb, vb, preferred_element_type=F32)
    chip = (sa + sb).astype(B16)
    in_quad = lax.all_gather(chip, "seq", axis=0, axis_index_groups=QUAD).astype(F32)
    total = jnp.sum(in_quad, axis=0)
    before = jnp.sum(jnp.where((jnp.arange(4) < quad_place)[:, None, None, None], in_quad, 0.0), axis=0)
    quads = lax.all_gather(total.astype(B16), "seq", axis=0, axis_index_groups=ACROSS).astype(F32)
    before = before + jnp.sum(jnp.where((jnp.arange(4) < quad)[:, None, None, None], quads, 0.0), axis=0)
    pa = (before + jnp.where(first, 0.0, sb)).astype(B16)
    pb = (before + jnp.where(first, sa, 0.0)).astype(B16)
    gain = lax.dynamic_slice_in_dim(norm_gain, core * DH, DH)

    def attend(q, k, v, p):
        s = jnp.einsum("std,sud->stu", q, k, preferred_element_type=F32)
        causal = lax.broadcasted_iota(jnp.int32, (128, 128), 0) >= lax.broadcasted_iota(jnp.int32, (128, 128), 1)
        s = jnp.where(causal, s, 0.0).astype(B16)
        attn = jnp.einsum("stu,sue->ste", s, v, preferred_element_type=F32)
        attn = attn + jnp.einsum("std,sde->ste", q, p, preferred_element_type=F32)
        scale = lax.rsqrt(jnp.mean(attn * attn, axis=-1, keepdims=True) + 1e-06)
        return (attn * scale * gain).astype(B16)

    oa = attend(qa, ka, va, pa)
    ob = attend(qb, kb, vb, pb)
    sib = lax.ppermute(ob, "seq", SIBLING)
    out = jnp.concatenate([jnp.where(first, oa, sib), jnp.where(first, sib, oa)], axis=-1)
    return lax.all_to_all(out, "dp", split_axis=0, concat_axis=2, tiled=True)


def solution(mesh):
    in_specs = (P("dp", "seq", None), P(None, "seq", ("heads", "dp")), P(("heads", "dp")))
    out_specs = P("dp", "seq", "heads")
    return jax.shard_map(body, mesh=mesh, in_specs=in_specs, out_specs=out_specs, check_vma=False)
```

```python
import jax
import jax.numpy as jnp
from jax import lax
from jax.experimental import pallas as pl
from jax.experimental.pallas import tpu as pltpu
from jax.sharding import PartitionSpec as P

DH = 128
SEQ = 32
BLOCK = 128
SEQS = 4
WSCALE = 2.0**19
F32 = jnp.float32
B16 = jnp.bfloat16
SAME_CORE = [[2 * z + c for z in range(16)] for c in range(2)]
SIBLING = [(i, i ^ 1) for i in range(SEQ)]
QUAD = [[8 * a + 2 * b + c for b in range(4)] for a in range(4) for c in range(2)]
ACROSS = [[8 * a + 2 * b + c for a in range(4)] for b in range(4) for c in range(2)]
OWNERS = [[(2 * z + c) * 4 + y for y in range(4) for c in range(2)] for z in range(16)]
VMEM = pl.BlockSpec(memory_space=pltpu.VMEM)
SMEM = pl.BlockSpec(memory_space=pltpu.SMEM)
PARAMS = pltpu.CompilerParams(vmem_limit_bytes=24 * 1024 * 1024)


def silu_b(v):
    return (v * jax.nn.sigmoid(v)).astype(B16)


def rows(s):
    return slice(s * BLOCK, (s + 1) * BLOCK)


def outer(k, v):
    return lax.dot_general(k, v, (((0,), (0,)), ((), ())), preferred_element_type=F32)


def first_kernel(t_ref, w_ref, q_ref, k_ref, v_ref, s_ref):
    t = t_ref[...]
    kv = jnp.dot(t, w_ref[:, DH:], preferred_element_type=F32)
    k_ref[...] = silu_b(kv[:, :DH])
    v_ref[...] = kv[:, DH:].astype(B16)
    q_ref[...] = silu_b(jnp.dot(t, w_ref[:, :DH], preferred_element_type=F32))
    for s in range(SEQS):
        s_ref[s] = outer(k_ref[rows(s)], v_ref[rows(s)])


def second_kernel(t_ref, w_ref, sa_ref, k_ref, v_ref, s_ref, chip_ref):
    kv = jnp.dot(t_ref[...], w_ref[:, DH:], preferred_element_type=F32)
    k_ref[...] = silu_b(kv[:, :DH])
    v_ref[...] = kv[:, DH:].astype(B16)
    for s in range(SEQS):
        state = outer(k_ref[rows(s)], v_ref[rows(s)])
        s_ref[s] = state
        chip_ref[s] = (sa_ref[s] + state).astype(B16)


def local(q, k, v):
    scores = lax.dot_general(q, k, (((1,), (1,)), ((), ())), preferred_element_type=F32)
    causal = lax.broadcasted_iota(jnp.int32, scores.shape, 0) >= lax.broadcasted_iota(jnp.int32, scores.shape, 1)
    return jnp.dot(jnp.where(causal, scores, 0.0).astype(B16), v, preferred_element_type=F32)


def local_kernel(t_ref, w_ref, qa_ref, ka_ref, va_ref, kb_ref, vb_ref, qb_ref, la_ref, lb_ref):
    qb_ref[...] = silu_b(jnp.dot(t_ref[...], w_ref[:, :DH], preferred_element_type=F32))
    for s in range(SEQS):
        r = rows(s)
        la_ref[r] = local(qa_ref[r], ka_ref[r], va_ref[r])
        lb_ref[r] = local(qb_ref[r], kb_ref[r], vb_ref[r])


def final_kernel(core_ref, qa_ref, qb_ref, la_ref, lb_ref, before_ref, sa_ref, sb_ref, gain_ref, o_ref):
    core = core_ref[0]
    gain = jnp.where(core == 0, gain_ref[0:1], gain_ref[1:2])

    def normed(q, l, p):
        attn = l + jnp.dot(q, p.astype(B16), preferred_element_type=F32)
        scale = lax.rsqrt(jnp.mean(attn * attn, axis=-1, keepdims=True) + 1e-06)
        return (attn * scale * gain).astype(B16)

    for s in range(SEQS):
        r = rows(s)
        before = before_ref[s].astype(F32)
        pa = jnp.where(core == 0, before, before + sb_ref[s])
        pb = jnp.where(core == 0, before + sa_ref[s], before)
        o_ref[s, core] = normed(qa_ref[r], la_ref[r], pa)
        o_ref[s, 1 - core] = normed(qb_ref[r], lb_ref[r], pb)


def call(kernel, name, outs, *args):
    return pl.pallas_call(
        kernel,
        name=name,
        out_shape=[jax.ShapeDtypeStruct(s, d) for s, d in outs],
        in_specs=[SMEM if a.dtype == jnp.int32 else VMEM for a in args],
        out_specs=[VMEM for _ in outs],
        compiler_params=PARAMS,
    )(*args)


def body(tokens, proj_weights, norm_gain):
    place = lax.axis_index("seq")
    core = place & 1
    quad = place >> 3
    mine_t = lax.all_to_all(jnp.broadcast_to(tokens, (SEQS,) + tokens.shape[1:]), "dp", 0, 0, tiled=True)
    wh = (proj_weights.astype(F32) * WSCALE).astype(jnp.float16)
    wh = jnp.transpose(wh, (1, 0, 2)).reshape(-1, 3, 2, DH)
    head0, head1 = wh[:, :, 0].reshape(-1, 3 * DH), wh[:, :, 1].reshape(-1, 3 * DH)
    first = core == 0
    keep = jnp.where(first, head0, head1)
    give = jnp.where(first, head1, head0)
    got = lax.ppermute(give, "seq", SIBLING)
    pair = jnp.concatenate([jnp.where(first, keep, got), jnp.where(first, got, keep)], axis=0)
    full = lax.all_gather(pair, "seq", axis=0, tiled=True, axis_index_groups=SAME_CORE)
    mine_t, full = lax.optimization_barrier((mine_t, full))
    other_t = lax.ppermute(mine_t, "seq", SIBLING)
    weights = (full.astype(F32) * (1.0 / WSCALE)).astype(B16)
    n = SEQS * BLOCK
    ta, tb = mine_t.reshape(n, -1), other_t.reshape(n, -1)
    block, state = ((n, DH), B16), ((SEQS, DH, DH), F32)
    qa, ka, va, sa = call(first_kernel, "first", [block, block, block, state], ta, weights)
    kb, vb, sb, chip = call(second_kernel, "second", [block, block, state, ((SEQS, DH, DH), B16)], tb, weights, sa)

    by_chip = lax.all_to_all(chip, "seq", 0, 0, tiled=True, axis_index_groups=QUAD).astype(F32)
    total = jnp.sum(by_chip, axis=0).astype(B16)
    totals = lax.all_gather(total, "seq", axis=0, axis_index_groups=ACROSS).astype(F32)
    before = jnp.sum(jnp.where((jnp.arange(4) < quad)[:, None, None], totals, 0.0), axis=0)
    parts = [before]
    for j in range(3):
        parts.append(parts[-1] + by_chip[j])
    back = lax.all_to_all(jnp.stack(parts).astype(B16), "seq", 0, 0, tiled=True, axis_index_groups=QUAD)

    qb, la, lb = call(local_kernel, "local", [block, ((n, DH), F32), ((n, DH), F32)], tb, weights, qa, ka, va, kb, vb)
    (out,) = call(
        final_kernel, "final", [((SEQS, 2, BLOCK, DH), B16)],
        core.reshape(1), qa, qb, la, lb, back, sa, sb, norm_gain.reshape(2, DH),
    )
    out = lax.all_to_all(out.reshape(8, BLOCK, DH), ("seq", "dp"), 0, 0, tiled=True, axis_index_groups=OWNERS)
    return jnp.transpose(out, (1, 0, 2)).reshape(1, BLOCK, 8 * DH)


def solution(mesh):
    in_specs = (P("dp", "seq", None), P(None, "seq", ("heads", "dp")), P(("heads", "dp")))
    out_specs = P("dp", "seq", "heads")
    return jax.shard_map(body, mesh=mesh, in_specs=in_specs, out_specs=out_specs, check_vma=False)
```

```python
import jax
import jax.numpy as jnp
from jax import lax
from jax.experimental import pallas as pl
from jax.experimental.pallas import tpu as pltpu
from jax.sharding import PartitionSpec as P

DH = 128
SEQ = 32
BLOCK = 128
SEQS = 4
WSCALE = 2.0**19
F32 = jnp.float32
B16 = jnp.bfloat16
SAME_CORE = [[2 * z + c for z in range(16)] for c in range(2)]
SIBLING = [(i, i ^ 1) for i in range(SEQ)]
QUAD = [[8 * a + 2 * b + c for b in range(4)] for a in range(4) for c in range(2)]
ACROSS = [[8 * a + 2 * b + c for a in range(4)] for b in range(4) for c in range(2)]
OWNERS = [[(2 * z + c) * 4 + y for y in range(4) for c in range(2)] for z in range(16)]
VMEM = pl.BlockSpec(memory_space=pltpu.VMEM)
SMEM = pl.BlockSpec(memory_space=pltpu.SMEM)
PARAMS = pltpu.CompilerParams(vmem_limit_bytes=24 * 1024 * 1024)


def silu_b(v):
    return (v * jax.nn.sigmoid(v)).astype(B16)


def rows(s):
    return slice(s * BLOCK, (s + 1) * BLOCK)


def outer(k, v):
    return lax.dot_general(k, v, (((0,), (0,)), ((), ())), preferred_element_type=F32)


def local(q, k, v):
    scores = lax.dot_general(q, k, (((1,), (1,)), ((), ())), preferred_element_type=F32)
    causal = lax.broadcasted_iota(jnp.int32, scores.shape, 0) >= lax.broadcasted_iota(jnp.int32, scores.shape, 1)
    return jnp.dot(jnp.where(causal, scores, 0.0).astype(B16), v, preferred_element_type=F32)


def block_work(t_ref, w_ref, q_ref, l_ref, s_ref):
    out = jnp.dot(t_ref[...], w_ref[...], preferred_element_type=F32)
    q, k, v = silu_b(out[:, :DH]), silu_b(out[:, DH : 2 * DH]), out[:, 2 * DH :].astype(B16)
    q_ref[...] = q
    for s in range(SEQS):
        r = rows(s)
        s_ref[s] = outer(k[r], v[r])
        l_ref[r] = local(q[r], k[r], v[r])


def first_kernel(t_ref, w_ref, q_ref, l_ref, s_ref):
    block_work(t_ref, w_ref, q_ref, l_ref, s_ref)


def second_kernel(t_ref, w_ref, sa_ref, q_ref, l_ref, s_ref, chip_ref):
    block_work(t_ref, w_ref, q_ref, l_ref, s_ref)
    for s in range(SEQS):
        chip_ref[s] = (sa_ref[s] + s_ref[s]).astype(B16)


def copies_kernel(t_ref, o_ref, sem):
    copies = [pltpu.make_async_copy(t_ref, o_ref.at[s], sem.at[s]) for s in range(SEQS)]
    for c in copies:
        c.start()
    for c in copies:
        c.wait()


def final_kernel(core_ref, qa_ref, qb_ref, la_ref, lb_ref, before_ref, sa_ref, sb_ref, gain_ref, o_ref):
    core = core_ref[0]
    gain = jnp.where(core == 0, gain_ref[0:1], gain_ref[1:2])

    def normed(q, l, p):
        attn = l + jnp.dot(q, p.astype(B16), preferred_element_type=F32)
        scale = lax.rsqrt(jnp.mean(attn * attn, axis=-1, keepdims=True) + 1e-06)
        return (attn * scale * gain).astype(B16)

    for s in range(SEQS):
        r = rows(s)
        before = before_ref[s].astype(F32)
        pa = jnp.where(core == 0, before, before + sb_ref[s])
        pb = jnp.where(core == 0, before + sa_ref[s], before)
        o_ref[s, core] = normed(qa_ref[r], la_ref[r], pa)
        o_ref[s, 1 - core] = normed(qb_ref[r], lb_ref[r], pb)


def call(kernel, name, outs, *args):
    return pl.pallas_call(
        kernel,
        name=name,
        out_shape=[jax.ShapeDtypeStruct(s, d) for s, d in outs],
        in_specs=[SMEM if a.dtype == jnp.int32 else VMEM for a in args],
        out_specs=[VMEM for _ in outs],
        compiler_params=PARAMS,
    )(*args)


def body(tokens, proj_weights, norm_gain):
    place = lax.axis_index("seq")
    core = place & 1
    quad = place >> 3
    first = core == 0
    wh = (proj_weights.astype(F32) * WSCALE).astype(jnp.float16)
    wh = jnp.transpose(wh, (1, 0, 2)).reshape(-1, 3, 2, DH)
    head0, head1 = wh[:, :, 0].reshape(-1, 3 * DH), wh[:, :, 1].reshape(-1, 3 * DH)
    keep = jnp.where(first, head0, head1)
    give = jnp.where(first, head1, head0)
    got = lax.ppermute(give, "seq", SIBLING)
    hbm = pl.BlockSpec(memory_space=pl.ANY)
    copies = pl.pallas_call(
        copies_kernel,
        name="copies",
        out_shape=jax.ShapeDtypeStruct((SEQS,) + tokens.shape[1:], B16),
        in_specs=[hbm],
        out_specs=hbm,
        scratch_shapes=[pltpu.SemaphoreType.DMA((SEQS,))],
    )(tokens[0])
    copies, got = lax.optimization_barrier((copies, got))
    mine_t = lax.all_to_all(copies, "dp", 0, 0, tiled=True)
    pair = jnp.concatenate([jnp.where(first, keep, got), jnp.where(first, got, keep)], axis=0)
    full = lax.all_gather(pair, "seq", axis=0, tiled=True, axis_index_groups=SAME_CORE)
    mine_t, full = lax.optimization_barrier((mine_t, full))
    other_t = lax.ppermute(mine_t, "seq", SIBLING)
    weights = (full.astype(F32) * (1.0 / WSCALE)).astype(B16)
    n = SEQS * BLOCK
    ta, tb = mine_t.reshape(n, -1), other_t.reshape(n, -1)
    outs = [((n, DH), B16), ((n, DH), F32), ((SEQS, DH, DH), F32)]
    qa, la, sa = call(first_kernel, "first", outs, ta, weights)
    qb, lb, sb, chip = call(second_kernel, "second", outs + [((SEQS, DH, DH), B16)], tb, weights, sa)
    chip, qa, la, sa, qb, lb, sb = lax.optimization_barrier((chip, qa, la, sa, qb, lb, sb))

    by_chip = lax.all_to_all(chip, "seq", 0, 0, tiled=True, axis_index_groups=QUAD).astype(F32)
    total = jnp.sum(by_chip, axis=0).astype(B16)
    totals = lax.all_gather(total, "seq", axis=0, axis_index_groups=ACROSS).astype(F32)
    before = jnp.sum(jnp.where((jnp.arange(4) < quad)[:, None, None], totals, 0.0), axis=0)
    parts = [before]
    for j in range(3):
        parts.append(parts[-1] + by_chip[j])
    back = lax.all_to_all(jnp.stack(parts).astype(B16), "seq", 0, 0, tiled=True, axis_index_groups=QUAD)
    (out,) = call(
        final_kernel, "final", [((SEQS, 2, BLOCK, DH), B16)],
        core.reshape(1), qa, qb, la, lb, back, sa, sb, norm_gain.reshape(2, DH),
    )
    out = lax.all_to_all(out.reshape(8, BLOCK, DH), ("seq", "dp"), 0, 0, tiled=True, axis_index_groups=OWNERS)
    return jnp.transpose(out, (1, 0, 2)).reshape(1, BLOCK, 8 * DH)


def solution(mesh):
    in_specs = (P("dp", "seq", None), P(None, "seq", ("heads", "dp")), P(("heads", "dp")))
    out_specs = P("dp", "seq", "heads")
    return jax.shard_map(body, mesh=mesh, in_specs=in_specs, out_specs=out_specs, check_vma=False)
```

```python
import jax
import jax.numpy as jnp
from jax import lax
from jax.experimental import pallas as pl
from jax.experimental.pallas import tpu as pltpu
from jax.sharding import PartitionSpec as P

DH = 128
SEQ = 32
BLOCK = 128
SEQS = 4
WSCALE = 2.0**19
F32 = jnp.float32
B16 = jnp.bfloat16
SAME_CORE = [[2 * z + c for z in range(16)] for c in range(2)]
SIBLING = [(i, i ^ 1) for i in range(SEQ)]
QUAD = [[8 * a + 2 * b + c for b in range(4)] for a in range(4) for c in range(2)]
ACROSS = [[8 * a + 2 * b + c for a in range(4)] for b in range(4) for c in range(2)]
OWNERS = [[(2 * z + c) * 4 + y for y in range(4) for c in range(2)] for z in range(16)]
VMEM = pl.BlockSpec(memory_space=pltpu.VMEM)
SMEM = pl.BlockSpec(memory_space=pltpu.SMEM)
PARAMS = pltpu.CompilerParams(vmem_limit_bytes=24 * 1024 * 1024)


def silu_b(v):
    return (v * jax.nn.sigmoid(v)).astype(B16)


def rows(s):
    return slice(s * BLOCK, (s + 1) * BLOCK)


def outer(k, v):
    return lax.dot_general(k, v, (((0,), (0,)), ((), ())), preferred_element_type=F32)


def local(q, k, v):
    scores = lax.dot_general(q, k, (((1,), (1,)), ((), ())), preferred_element_type=F32)
    causal = lax.broadcasted_iota(jnp.int32, scores.shape, 0) >= lax.broadcasted_iota(jnp.int32, scores.shape, 1)
    return jnp.dot(jnp.where(causal, scores, 0.0).astype(B16), v, preferred_element_type=F32)


def block_work(t_ref, w_ref, q_ref, l_ref, s_ref):
    out = jnp.dot(t_ref[...], w_ref[...], preferred_element_type=F32)
    q, k, v = silu_b(out[:, :DH]), silu_b(out[:, DH : 2 * DH]), out[:, 2 * DH :].astype(B16)
    q_ref[...] = q
    for s in range(SEQS):
        r = rows(s)
        s_ref[s] = outer(k[r], v[r])
        l_ref[r] = local(q[r], k[r], v[r])


def first_kernel(t_ref, w_ref, q_ref, l_ref, s_ref):
    block_work(t_ref, w_ref, q_ref, l_ref, s_ref)


def second_kernel(t_ref, w_ref, sa_ref, q_ref, l_ref, s_ref, chip_ref):
    block_work(t_ref, w_ref, q_ref, l_ref, s_ref)
    for s in range(SEQS):
        chip_ref[s] = (sa_ref[s] + s_ref[s]).astype(B16)


def total_kernel(r_ref, o_ref):
    o_ref[...] = (r_ref[0].astype(F32) + r_ref[1].astype(F32) + r_ref[2].astype(F32) + r_ref[3].astype(F32)).astype(B16)


def parts_kernel(quad_ref, r_ref, totals_ref, o_ref):
    quad = quad_ref[0]
    before = jnp.zeros((DH, DH), F32)
    for a in range(3):
        before = before + jnp.where(a < quad, totals_ref[a].astype(F32), 0.0)
    o_ref[0] = before.astype(B16)
    for j in range(3):
        before = before + r_ref[j].astype(F32)
        o_ref[j + 1] = before.astype(B16)


def copies_kernel(t_ref, o_ref, sem):
    copies = [pltpu.make_async_copy(t_ref, o_ref.at[s], sem.at[s]) for s in range(SEQS)]
    for c in copies:
        c.start()
    for c in copies:
        c.wait()


def final_kernel(core_ref, qa_ref, qb_ref, la_ref, lb_ref, before_ref, sa_ref, sb_ref, gain_ref, o_ref):
    core = core_ref[0]
    gain = jnp.where(core == 0, gain_ref[0:1], gain_ref[1:2])

    def normed(q, l, p):
        attn = l + jnp.dot(q, p.astype(B16), preferred_element_type=F32)
        scale = lax.rsqrt(jnp.mean(attn * attn, axis=-1, keepdims=True) + 1e-06)
        return (attn * scale * gain).astype(B16)

    for s in range(SEQS):
        r = rows(s)
        before = before_ref[s].astype(F32)
        pa = jnp.where(core == 0, before, before + sb_ref[s])
        pb = jnp.where(core == 0, before + sa_ref[s], before)
        o_ref[s, core] = normed(qa_ref[r], la_ref[r], pa)
        o_ref[s, 1 - core] = normed(qb_ref[r], lb_ref[r], pb)


def call(kernel, name, outs, *args):
    return pl.pallas_call(
        kernel,
        name=name,
        out_shape=[jax.ShapeDtypeStruct(s, d) for s, d in outs],
        in_specs=[SMEM if a.dtype == jnp.int32 else VMEM for a in args],
        out_specs=[VMEM for _ in outs],
        compiler_params=PARAMS,
    )(*args)


def body(tokens, proj_weights, norm_gain):
    place = lax.axis_index("seq")
    core = place & 1
    quad = (place >> 3).reshape(1)
    first = core == 0
    wh = (proj_weights.astype(F32) * WSCALE).astype(jnp.float16)
    wh = jnp.transpose(wh, (1, 0, 2)).reshape(-1, 3, 2, DH)
    head0, head1 = wh[:, :, 0].reshape(-1, 3 * DH), wh[:, :, 1].reshape(-1, 3 * DH)
    keep = jnp.where(first, head0, head1)
    give = jnp.where(first, head1, head0)
    got = lax.ppermute(give, "seq", SIBLING)
    copies = pl.pallas_call(
        copies_kernel,
        name="copies",
        out_shape=jax.ShapeDtypeStruct((SEQS,) + tokens.shape[1:], B16),
        in_specs=[VMEM],
        out_specs=pl.BlockSpec(memory_space=pl.ANY),
        scratch_shapes=[pltpu.SemaphoreType.DMA((SEQS,))],
    )(tokens[0])
    copies, got = lax.optimization_barrier((copies, got))
    mine_t = lax.all_to_all(copies, "dp", 0, 0, tiled=True)
    pair = jnp.concatenate([jnp.where(first, keep, got), jnp.where(first, got, keep)], axis=0)
    full = lax.all_gather(pair, "seq", axis=0, tiled=True, axis_index_groups=SAME_CORE)
    mine_t, full = lax.optimization_barrier((mine_t, full))
    other_t = lax.ppermute(mine_t, "seq", SIBLING)
    weights = (full.astype(F32) * (1.0 / WSCALE)).astype(B16)
    n = SEQS * BLOCK
    ta, tb = mine_t.reshape(n, -1), other_t.reshape(n, -1)
    outs = [((n, DH), B16), ((n, DH), F32), ((SEQS, DH, DH), F32)]
    qa, la, sa = call(first_kernel, "first", outs, ta, weights)
    qb, lb, sb, chip = call(second_kernel, "second", outs + [((SEQS, DH, DH), B16)], tb, weights, sa)
    chip, qa, la, sa, qb, lb, sb, quad = lax.optimization_barrier((chip, qa, la, sa, qb, lb, sb, quad))

    square = (DH, DH)
    by_chip = lax.all_to_all(chip, "seq", 0, 0, tiled=True, axis_index_groups=QUAD)
    (total,) = call(total_kernel, "total", [(square, B16)], by_chip)
    totals = lax.all_gather(total, "seq", axis=0, axis_index_groups=ACROSS)
    (parts,) = call(parts_kernel, "parts", [((4,) + square, B16)], quad, by_chip, totals)
    back = lax.all_to_all(parts, "seq", 0, 0, tiled=True, axis_index_groups=QUAD)
    (out,) = call(
        final_kernel, "final", [((SEQS, 2, BLOCK, DH), B16)],
        core.reshape(1), qa, qb, la, lb, back, sa, sb, norm_gain.reshape(2, DH),
    )
    out = lax.all_to_all(out.reshape(8, BLOCK, DH), ("seq", "dp"), 0, 0, tiled=True, axis_index_groups=OWNERS)
    return jnp.transpose(out, (1, 0, 2)).reshape(1, BLOCK, 8 * DH)


def solution(mesh):
    in_specs = (P("dp", "seq", None), P(None, "seq", ("heads", "dp")), P(("heads", "dp")))
    out_specs = P("dp", "seq", "heads")
    return jax.shard_map(body, mesh=mesh, in_specs=in_specs, out_specs=out_specs, check_vma=False)
```

```python
import jax
import jax.numpy as jnp
from jax import lax
from jax.experimental import pallas as pl
from jax.experimental.pallas import tpu as pltpu
from jax.sharding import PartitionSpec as P

DH = 128
SEQ = 32
BLOCK = 128
SEQS = 4
WSCALE = 2.0**19
F32 = jnp.float32
B16 = jnp.bfloat16
SIBLING = [(i, i ^ 1) for i in range(SEQ)]
QUAD = [[8 * a + 2 * b + c for b in range(4)] for a in range(4) for c in range(2)]


def holder(z, head):
    return 2 * z + (head ^ ((z >> 2) & 1))


SAME_HEAD = [[holder(z, h) for z in range(16)] for h in range(2)]
ACROSS = [[holder(4 * a + b, h) for a in range(4)] for b in range(4) for h in range(2)]
OWNERS = [[holder(z, h) * 4 + y for y in range(4) for h in range(2)] for z in range(16)]
VMEM = pl.BlockSpec(memory_space=pltpu.VMEM)
SMEM = pl.BlockSpec(memory_space=pltpu.SMEM)
PARAMS = pltpu.CompilerParams(vmem_limit_bytes=24 * 1024 * 1024)


def silu_b(v):
    return (v * jax.nn.sigmoid(v)).astype(B16)


def rows(s):
    return slice(s * BLOCK, (s + 1) * BLOCK)


def outer(k, v):
    return lax.dot_general(k, v, (((0,), (0,)), ((), ())), preferred_element_type=F32)


def local(q, k, v):
    scores = lax.dot_general(q, k, (((1,), (1,)), ((), ())), preferred_element_type=F32)
    causal = lax.broadcasted_iota(jnp.int32, scores.shape, 0) >= lax.broadcasted_iota(jnp.int32, scores.shape, 1)
    return jnp.dot(jnp.where(causal, scores, 0.0).astype(B16), v, preferred_element_type=F32)


def block_work(out, q_ref, l_ref, s_ref):
    q, k, v = silu_b(out[:, :DH]), silu_b(out[:, DH : 2 * DH]), out[:, 2 * DH :].astype(B16)
    q_ref[...] = q
    for s in range(SEQS):
        r = rows(s)
        s_ref[s] = outer(k[r], v[r])
        l_ref[r] = local(q[r], k[r], v[r])


def first_kernel(t_ref, w_ref, q_ref, l_ref, s_ref):
    block_work(jnp.dot(t_ref[...], w_ref[...], preferred_element_type=F32), q_ref, l_ref, s_ref)


def second_kernel(t_ref, w_ref, sa_ref, q_ref, l_ref, s_ref, chip_ref, piece, acc, sem):
    count, _, width = piece.shape
    span = [slice(i * width, (i + 1) * width) for i in range(count)]
    copies = [pltpu.make_async_copy(t_ref.at[:, span[i]], piece.at[i], sem.at[i]) for i in range(count)]
    for c in copies:
        c.start()
    for i in range(count):
        copies[i].wait()
        part = jnp.dot(piece[i], w_ref[span[i]], preferred_element_type=F32)
        if i == 0:
            acc[...] = part
        else:
            acc[...] += part
    block_work(acc[...], q_ref, l_ref, s_ref)
    for s in range(SEQS):
        chip_ref[s] = (sa_ref[s] + s_ref[s]).astype(B16)


def total_kernel(r_ref, o_ref):
    o_ref[...] = (r_ref[0].astype(F32) + r_ref[1].astype(F32) + r_ref[2].astype(F32) + r_ref[3].astype(F32)).astype(B16)


def parts_kernel(quad_ref, r_ref, totals_ref, o_ref):
    quad = quad_ref[0]
    before = jnp.zeros((DH, DH), F32)
    for a in range(3):
        before = before + jnp.where(a < quad, totals_ref[a].astype(F32), 0.0)
    o_ref[0] = before.astype(B16)
    for j in range(3):
        before = before + r_ref[j].astype(F32)
        o_ref[j + 1] = before.astype(B16)


def copies_kernel(t_ref, o_ref, buf, sem_in, sem):
    count = buf.shape[0]
    loads = [pltpu.make_async_copy(t_ref.at[pl.ds(i * 32, 32)], buf.at[i], sem_in.at[i]) for i in range(count)]
    stores = [
        pltpu.make_async_copy(buf.at[i], o_ref.at[s, pl.ds(i * 32, 32)], sem.at[i, s])
        for i in range(count) for s in range(SEQS)
    ]
    for c in loads:
        c.start()
    for i in range(count):
        loads[i].wait()
        for c in stores[i * SEQS : (i + 1) * SEQS]:
            c.start()
    for c in stores:
        c.wait()


def join_kernel(i_ref, o_ref, sem):
    count = i_ref.shape[0]
    copies = [pltpu.make_async_copy(i_ref.at[j], o_ref.at[:, pl.ds(j * DH, DH)], sem.at[j]) for j in range(count)]
    for c in copies:
        c.start()
    for c in copies:
        c.wait()


def final_kernel(spot_ref, qa_ref, qb_ref, la_ref, lb_ref, before_ref, sa_ref, sb_ref, gain_ref, o_ref):
    core, head = spot_ref[0], spot_ref[1]
    gain = jnp.where(head == 0, gain_ref[0:1], gain_ref[1:2])

    def normed(q, l, p):
        attn = l + jnp.dot(q, p.astype(B16), preferred_element_type=F32)
        scale = lax.rsqrt(jnp.mean(attn * attn, axis=-1, keepdims=True) + 1e-06)
        return (attn * scale * gain).astype(B16)

    for s in range(SEQS):
        r = rows(s)
        before = before_ref[s].astype(F32)
        pa = jnp.where(core == 0, before, before + sb_ref[s])
        pb = jnp.where(core == 0, before + sa_ref[s], before)
        o_ref[s, head] = normed(qa_ref[r], la_ref[r], pa)
        o_ref[s, 1 - head] = normed(qb_ref[r], lb_ref[r], pb)


def call(kernel, name, outs, *args, away=(), out_away=False, scratch=()):
    anywhere = pl.BlockSpec(memory_space=pltpu.HBM if out_away else pl.ANY)
    return pl.pallas_call(
        kernel,
        name=name,
        out_shape=[jax.ShapeDtypeStruct(s, d) for s, d in outs],
        in_specs=[SMEM if a.dtype == jnp.int32 else anywhere if i in away else VMEM for i, a in enumerate(args)],
        out_specs=[anywhere if out_away else VMEM for _ in outs],
        scratch_shapes=list(scratch),
        compiler_params=PARAMS,
    )(*args)


def body(tokens, proj_weights, norm_gain):
    place = lax.axis_index("seq")
    core = place & 1
    quad = place >> 3
    head = core ^ (quad & 1)
    spot = jnp.stack([core, head])
    quad = quad.reshape(1)
    wh = (proj_weights.astype(F32) * WSCALE).astype(jnp.float16)
    wh = jnp.transpose(wh, (1, 0, 2)).reshape(-1, 3, 2, DH)
    head0, head1 = wh[:, :, 0].reshape(-1, 3 * DH), wh[:, :, 1].reshape(-1, 3 * DH)
    keep = jnp.where(head == 0, head0, head1)
    give = jnp.where(head == 0, head1, head0)
    got = lax.ppermute(give, "seq", SIBLING)
    (copies,) = call(
        copies_kernel, "copies", [((SEQS,) + tokens.shape[1:], B16)], tokens[0], away=(0,), out_away=True,
        scratch=[pltpu.VMEM((4, 32) + tokens.shape[2:], B16), pltpu.SemaphoreType.DMA((4,)), pltpu.SemaphoreType.DMA((4, SEQS))],
    )
    copies, got = lax.optimization_barrier((copies, got))
    mine_t = lax.all_to_all(copies, "dp", 0, 0, tiled=True)
    first = core == 0
    pair = jnp.concatenate([jnp.where(first, keep, got), jnp.where(first, got, keep)], axis=0)
    full = lax.all_gather(pair, "seq", axis=0, tiled=True, axis_index_groups=SAME_HEAD)
    mine_t, full = lax.optimization_barrier((mine_t, full))
    other_t = lax.ppermute(mine_t, "seq", SIBLING)
    weights = (full.astype(F32) * (1.0 / WSCALE)).astype(B16)
    n = SEQS * BLOCK
    ta, tb = mine_t.reshape(n, -1), other_t.reshape(n, -1)
    outs = [((n, DH), B16), ((n, DH), F32), ((SEQS, DH, DH), F32)]
    qa, la, sa = call(first_kernel, "first", outs, ta, weights)
    width = tb.shape[1] // 4
    qb, lb, sb, chip = call(
        second_kernel, "second", outs + [((SEQS, DH, DH), B16)], tb, weights, sa, away=(0,),
        scratch=[pltpu.VMEM((4, n, width), B16), pltpu.VMEM((n, 3 * DH), F32), pltpu.SemaphoreType.DMA((4,))],
    )
    chip, qa, la, sa, qb, lb, sb, quad, spot = lax.optimization_barrier((chip, qa, la, sa, qb, lb, sb, quad, spot))

    square = (DH, DH)
    by_chip = lax.all_to_all(chip, "seq", 0, 0, tiled=True, axis_index_groups=QUAD)
    (total,) = call(total_kernel, "total", [(square, B16)], by_chip)
    totals = lax.all_gather(total, "seq", axis=0, axis_index_groups=ACROSS)
    (parts,) = call(parts_kernel, "parts", [((4,) + square, B16)], quad, by_chip, totals)
    back = lax.all_to_all(parts, "seq", 0, 0, tiled=True, axis_index_groups=QUAD)
    (out,) = call(
        final_kernel, "final", [((SEQS, 2, BLOCK, DH), B16)],
        spot, qa, qb, la, lb, back, sa, sb, norm_gain.reshape(2, DH),
    )
    out = lax.all_to_all(out.reshape(8, BLOCK, DH), ("seq", "dp"), 0, 0, tiled=True, axis_index_groups=OWNERS)
    (joined,) = call(
        join_kernel, "join", [((BLOCK, 8 * DH), B16)], out, out_away=True, scratch=[pltpu.SemaphoreType.DMA((8,))]
    )
    return joined[None]


def solution(mesh):
    in_specs = (P("dp", "seq", None), P(None, "seq", ("heads", "dp")), P(("heads", "dp")))
    out_specs = P("dp", "seq", "heads")
    return jax.shard_map(body, mesh=mesh, in_specs=in_specs, out_specs=out_specs, check_vma=False)
```

```python
import jax
import jax.numpy as jnp
from jax import lax
from jax.experimental import pallas as pl
from jax.experimental.pallas import tpu as pltpu
from jax.sharding import PartitionSpec as P

DH = 128
SEQ = 32
BLOCK = 128
SEQS = 4
WSCALE = 2.0**19
F32 = jnp.float32
B16 = jnp.bfloat16
SIBLING = [(i, i ^ 1) for i in range(SEQ)]


def holder(z, head):
    return 2 * z + (head ^ ((z ^ (z >> 2)) & 1))


QUAD = [[holder(4 * a + b, h) for b in range(4)] for a in range(4) for h in range(2)]
def head_of(place):
    return (place ^ (place >> 1) ^ (place >> 3)) & 1


SAME_HEAD = [[holder(z, h) for z in range(16)] for h in range(2)]
ACROSS = [[holder(4 * a + b, h) for a in range(4)] for b in range(4) for h in range(2)]
OWNERS = [[holder(z, h) * 4 + y for y in range(4) for h in range(2)] for z in range(16)]
VMEM = pl.BlockSpec(memory_space=pltpu.VMEM)
SMEM = pl.BlockSpec(memory_space=pltpu.SMEM)
PARAMS = pltpu.CompilerParams(vmem_limit_bytes=24 * 1024 * 1024)


def silu_b(v):
    return (v * jax.nn.sigmoid(v)).astype(B16)


def rows(s):
    return slice(s * BLOCK, (s + 1) * BLOCK)


def outer(k, v):
    return lax.dot_general(k, v, (((0,), (0,)), ((), ())), preferred_element_type=F32)


def local(q, k, v):
    scores = lax.dot_general(q, k, (((1,), (1,)), ((), ())), preferred_element_type=F32)
    causal = lax.broadcasted_iota(jnp.int32, scores.shape, 0) >= lax.broadcasted_iota(jnp.int32, scores.shape, 1)
    return jnp.dot(jnp.where(causal, scores, 0.0).astype(B16), v, preferred_element_type=F32)


def block_work(out, q_ref, l_ref, s_ref):
    q, k, v = silu_b(out[:, :DH]), silu_b(out[:, DH : 2 * DH]), out[:, 2 * DH :].astype(B16)
    q_ref[...] = q
    for s in range(SEQS):
        r = rows(s)
        s_ref[s] = outer(k[r], v[r])
        l_ref[r] = local(q[r], k[r], v[r])


def first_kernel(t_ref, w_ref, q_ref, l_ref, s_ref):
    block_work(jnp.dot(t_ref[...], w_ref[...], preferred_element_type=F32), q_ref, l_ref, s_ref)


def second_kernel(t_ref, w_ref, sa_ref, q_ref, l_ref, s_ref, chip_ref, piece, acc, sem):
    count, _, width = piece.shape
    span = [slice(i * width, (i + 1) * width) for i in range(count)]
    copies = [pltpu.make_async_copy(t_ref.at[:, span[i]], piece.at[i], sem.at[i]) for i in range(count)]
    for c in copies:
        c.start()
    for i in range(count):
        copies[i].wait()
        part = jnp.dot(piece[i], w_ref[span[i]], preferred_element_type=F32)
        if i == 0:
            acc[...] = part
        else:
            acc[...] += part
    block_work(acc[...], q_ref, l_ref, s_ref)
    for s in range(SEQS):
        chip_ref[s] = (sa_ref[s] + s_ref[s]).astype(B16)


def total_kernel(r_ref, o_ref):
    o_ref[...] = (r_ref[0].astype(F32) + r_ref[1].astype(F32) + r_ref[2].astype(F32) + r_ref[3].astype(F32)).astype(B16)


def parts_kernel(spot_ref, r_ref, totals_ref, o_ref):
    quad = spot_ref[0] >> 3
    before = jnp.zeros((DH, DH), F32)
    for a in range(3):
        before = before + jnp.where(a < quad, totals_ref[a].astype(F32), 0.0)
    o_ref[0] = before.astype(B16)
    for j in range(3):
        before = before + r_ref[j].astype(F32)
        o_ref[j + 1] = before.astype(B16)


def copies_kernel(t_ref, o_ref, sem):
    copies = [pltpu.make_async_copy(t_ref, o_ref.at[s], sem.at[s]) for s in range(SEQS)]
    for c in copies:
        c.start()
    for c in copies:
        c.wait()


def join_kernel(i_ref, o_ref, sem):
    count = i_ref.shape[0]
    copies = [pltpu.make_async_copy(i_ref.at[j], o_ref.at[:, pl.ds(j * DH, DH)], sem.at[j]) for j in range(count)]
    for c in copies:
        c.start()
    for c in copies:
        c.wait()


def final_kernel(spot_ref, qa_ref, qb_ref, la_ref, lb_ref, before_ref, sa_ref, sb_ref, gain_ref, o_ref):
    core, head = spot_ref[0] & 1, head_of(spot_ref[0])
    gain = jnp.where(head == 0, gain_ref[0:1], gain_ref[1:2])

    def normed(q, l, p):
        attn = l + jnp.dot(q, p.astype(B16), preferred_element_type=F32)
        scale = lax.rsqrt(jnp.mean(attn * attn, axis=-1, keepdims=True) + 1e-06)
        return (attn * scale * gain).astype(B16)

    for s in range(SEQS):
        r = rows(s)
        before = before_ref[s].astype(F32)
        pa = jnp.where(core == 0, before, before + sb_ref[s])
        pb = jnp.where(core == 0, before + sa_ref[s], before)
        o_ref[s, head] = normed(qa_ref[r], la_ref[r], pa)
        o_ref[s, 1 - head] = normed(qb_ref[r], lb_ref[r], pb)


def call(kernel, name, outs, *args, away=(), out_away=False, scratch=(), params=True):
    anywhere = pl.BlockSpec(memory_space=pl.ANY)
    return pl.pallas_call(
        kernel,
        name=name,
        out_shape=[jax.ShapeDtypeStruct(s, d) for s, d in outs],
        in_specs=[SMEM if a.dtype == jnp.int32 else anywhere if i in away else VMEM for i, a in enumerate(args)],
        out_specs=[anywhere if out_away else VMEM for _ in outs],
        scratch_shapes=list(scratch),
        compiler_params=PARAMS if params else None,
    )(*args)


def body(tokens, proj_weights, norm_gain):
    place = lax.axis_index("seq")
    core = place & 1
    head = head_of(place)
    spot = place.reshape(1)
    wh = (proj_weights.astype(F32) * WSCALE).astype(jnp.float16)
    wh = jnp.transpose(wh, (1, 0, 2)).reshape(-1, 3, 2, DH)
    head0, head1 = wh[:, :, 0].reshape(-1, 3 * DH), wh[:, :, 1].reshape(-1, 3 * DH)
    keep = jnp.where(head == 0, head0, head1)
    give = jnp.where(head == 0, head1, head0)
    got = lax.ppermute(give, "seq", SIBLING)
    (copies,) = call(
        copies_kernel, "copies", [((SEQS,) + tokens.shape[1:], B16)], tokens[0], out_away=True, params=False,
        scratch=[pltpu.SemaphoreType.DMA((SEQS,))],
    )
    copies, got = lax.optimization_barrier((copies, got))
    mine_t = lax.all_to_all(copies, "dp", 0, 0, tiled=True)
    first = core == 0
    pair = jnp.concatenate([jnp.where(first, keep, got), jnp.where(first, got, keep)], axis=0)
    full = lax.all_gather(pair, "seq", axis=0, tiled=True, axis_index_groups=SAME_HEAD)
    mine_t, full = lax.optimization_barrier((mine_t, full))
    other_t = lax.ppermute(mine_t, "seq", SIBLING)
    weights = (full.astype(F32) * (1.0 / WSCALE)).astype(B16)
    n = SEQS * BLOCK
    ta, tb = mine_t.reshape(n, -1), other_t.reshape(n, -1)
    outs = [((n, DH), B16), ((n, DH), F32), ((SEQS, DH, DH), F32)]
    qa, la, sa = call(first_kernel, "first", outs, ta, weights)
    width = tb.shape[1] // 4
    qb, lb, sb, chip = call(
        second_kernel, "second", outs + [((SEQS, DH, DH), B16)], tb, weights, sa, away=(0,),
        scratch=[pltpu.VMEM((4, n, width), B16), pltpu.VMEM((n, 3 * DH), F32), pltpu.SemaphoreType.DMA((4,))],
    )
    chip, qa, la, sa, qb, lb, sb, spot = lax.optimization_barrier((chip, qa, la, sa, qb, lb, sb, spot))

    square = (DH, DH)
    by_chip = lax.all_to_all(chip, "seq", 0, 0, tiled=True, axis_index_groups=QUAD)
    (total,) = call(total_kernel, "total", [(square, B16)], by_chip)
    totals = lax.all_gather(total, "seq", axis=0, axis_index_groups=ACROSS)
    (parts,) = call(parts_kernel, "parts", [((4,) + square, B16)], spot, by_chip, totals)
    back = lax.all_to_all(parts, "seq", 0, 0, tiled=True, axis_index_groups=QUAD)
    (out,) = call(
        final_kernel, "final", [((SEQS, 2, BLOCK, DH), B16)],
        spot, qa, qb, la, lb, back, sa, sb, norm_gain.reshape(2, DH),
    )
    out = lax.all_to_all(out.reshape(8, BLOCK, DH), ("seq", "dp"), 0, 0, tiled=True, axis_index_groups=OWNERS)
    (joined,) = call(
        join_kernel, "join", [((BLOCK, 8 * DH), B16)], out, out_away=True, scratch=[pltpu.SemaphoreType.DMA((8,))]
    )
    return joined[None]


def solution(mesh):
    in_specs = (P("dp", "seq", None), P(None, "seq", ("heads", "dp")), P(("heads", "dp")))
    out_specs = P("dp", "seq", "heads")
    return jax.shard_map(body, mesh=mesh, in_specs=in_specs, out_specs=out_specs, check_vma=False)
```

```python
import jax
import jax.numpy as jnp
from jax import lax
from jax.experimental import pallas as pl
from jax.experimental.pallas import tpu as pltpu
from jax.sharding import PartitionSpec as P

DH = 128
SEQ = 32
BLOCK = 128
SEQS = 4
WSCALE = 2.0**19
F32 = jnp.float32
B16 = jnp.bfloat16
SIBLING = [(i, i ^ 1) for i in range(SEQ)]


def holder(z, head):
    return 2 * z + (head ^ ((z ^ (z >> 2)) & 1))


QUAD = [[holder(4 * a + b, h) for b in range(4)] for a in range(4) for h in range(2)]
def head_of(place):
    return (place ^ (place >> 1) ^ (place >> 3)) & 1


SAME_HEAD = [[holder(z, h) for z in range(16)] for h in range(2)]
ACROSS = [[holder(4 * a + b, h) for a in range(4)] for b in range(4) for h in range(2)]
OWNERS = [[holder(z, h) * 4 + y for y in range(4) for h in range(2)] for z in range(16)]
VMEM = pl.BlockSpec(memory_space=pltpu.VMEM)
SMEM = pl.BlockSpec(memory_space=pltpu.SMEM)
PARAMS = pltpu.CompilerParams(vmem_limit_bytes=24 * 1024 * 1024)


def silu_b(v):
    return (v * jax.nn.sigmoid(v)).astype(B16)


def rows(s):
    return slice(s * BLOCK, (s + 1) * BLOCK)


def outer(k, v):
    return lax.dot_general(k, v, (((0,), (0,)), ((), ())), preferred_element_type=F32)


def local(q, k, v):
    scores = lax.dot_general(q, k, (((1,), (1,)), ((), ())), preferred_element_type=F32)
    causal = lax.broadcasted_iota(jnp.int32, scores.shape, 0) >= lax.broadcasted_iota(jnp.int32, scores.shape, 1)
    return jnp.dot(jnp.where(causal, scores, 0.0).astype(B16), v, preferred_element_type=F32)


def block_work(out, q_ref, l_ref, s_ref):
    q, k, v = silu_b(out[:, :DH]), silu_b(out[:, DH : 2 * DH]), out[:, 2 * DH :].astype(B16)
    q_ref[...] = q
    for s in range(SEQS):
        r = rows(s)
        s_ref[s] = outer(k[r], v[r])
        l_ref[r] = local(q[r], k[r], v[r])


def first_kernel(t_ref, w_ref, q_ref, l_ref, s_ref):
    block_work(jnp.dot(t_ref[...], w_ref[...], preferred_element_type=F32), q_ref, l_ref, s_ref)


def second_kernel(t_ref, w_ref, sa_ref, q_ref, l_ref, s_ref, chip_ref):
    block_work(jnp.dot(t_ref[...], w_ref[...], preferred_element_type=F32), q_ref, l_ref, s_ref)
    for s in range(SEQS):
        chip_ref[s] = (sa_ref[s] + s_ref[s]).astype(B16)


def heads_kernel(spot_ref, w_ref, keep_ref, give_ref):
    mine = head_of(spot_ref[0]) == 0
    for j in range(3):
        low, high = w_ref[j, :, :DH], w_ref[j, :, DH:]
        keep_ref[:, j * DH : (j + 1) * DH] = jnp.where(mine, low, high)
        give_ref[:, j * DH : (j + 1) * DH] = jnp.where(mine, high, low)


def to_half(w):
    return (w.astype(F32) * WSCALE).astype(jnp.float16)


def total_kernel(r_ref, o_ref):
    o_ref[...] = (r_ref[0].astype(F32) + r_ref[1].astype(F32) + r_ref[2].astype(F32) + r_ref[3].astype(F32)).astype(B16)


def parts_kernel(spot_ref, r_ref, totals_ref, o_ref):
    quad = spot_ref[0] >> 3
    before = jnp.zeros((DH, DH), F32)
    for a in range(3):
        before = before + jnp.where(a < quad, totals_ref[a].astype(F32), 0.0)
    o_ref[0] = before.astype(B16)
    for j in range(3):
        before = before + r_ref[j].astype(F32)
        o_ref[j + 1] = before.astype(B16)


def copies_kernel(t_ref, o_ref, sem):
    copies = [pltpu.make_async_copy(t_ref, o_ref.at[s], sem.at[s]) for s in range(SEQS)]
    for c in copies:
        c.start()
    for c in copies:
        c.wait()


def join_kernel(i_ref, o_ref, sem):
    count = i_ref.shape[0]
    copies = [pltpu.make_async_copy(i_ref.at[j], o_ref.at[:, pl.ds(j * DH, DH)], sem.at[j]) for j in range(count)]
    for c in copies:
        c.start()
    for c in copies:
        c.wait()


def final_kernel(spot_ref, qa_ref, qb_ref, la_ref, lb_ref, before_ref, sa_ref, sb_ref, gain_ref, o_ref):
    core, head = spot_ref[0] & 1, head_of(spot_ref[0])
    gain = jnp.where(head == 0, gain_ref[0:1], gain_ref[1:2])

    def normed(q, l, p):
        attn = l + jnp.dot(q, p.astype(B16), preferred_element_type=F32)
        scale = lax.rsqrt(jnp.mean(attn * attn, axis=-1, keepdims=True) + 1e-06)
        return (attn * scale * gain).astype(B16)

    for s in range(SEQS):
        r = rows(s)
        before = before_ref[s].astype(F32)
        pa = jnp.where(core == 0, before, before + sb_ref[s])
        pb = jnp.where(core == 0, before + sa_ref[s], before)
        o_ref[s, head] = normed(qa_ref[r], la_ref[r], pa)
        o_ref[s, 1 - head] = normed(qb_ref[r], lb_ref[r], pb)


def call(kernel, name, outs, *args, away=(), out_away=False, scratch=(), params=True):
    anywhere = pl.BlockSpec(memory_space=pl.ANY)
    return pl.pallas_call(
        kernel,
        name=name,
        out_shape=[jax.ShapeDtypeStruct(s, d) for s, d in outs],
        in_specs=[SMEM if a.dtype == jnp.int32 else anywhere if i in away else VMEM for i, a in enumerate(args)],
        out_specs=[anywhere if out_away else VMEM for _ in outs],
        scratch_shapes=list(scratch),
        compiler_params=PARAMS if params else None,
    )(*args)


def body(tokens, proj_weights, norm_gain):
    place = lax.axis_index("seq")
    core = place & 1
    spot = place.reshape(1)
    own = ((proj_weights.shape[1], 3 * DH), B16)
    keep, give = call(heads_kernel, "heads", [own, own], spot, proj_weights)
    keep = to_half(keep)
    got = lax.ppermute(to_half(give), "seq", SIBLING)
    (copies,) = call(
        copies_kernel, "copies", [((SEQS,) + tokens.shape[1:], B16)], tokens[0], out_away=True, params=False,
        scratch=[pltpu.SemaphoreType.DMA((SEQS,))],
    )
    copies, got = lax.optimization_barrier((copies, got))
    mine_t = lax.all_to_all(copies, "dp", 0, 0, tiled=True)
    first = core == 0
    pair = jnp.concatenate([jnp.where(first, keep, got), jnp.where(first, got, keep)], axis=0)
    full = lax.all_gather(pair, "seq", axis=0, tiled=True, axis_index_groups=SAME_HEAD)
    weights = (full.astype(F32) * (1.0 / WSCALE)).astype(B16)
    mine_t, weights = lax.optimization_barrier((mine_t, weights))
    other_t = lax.ppermute(mine_t, "seq", SIBLING)
    n = SEQS * BLOCK
    ta, tb = mine_t.reshape(n, -1), other_t.reshape(n, -1)
    outs = [((n, DH), B16), ((n, DH), F32), ((SEQS, DH, DH), F32)]
    qa, la, sa = call(first_kernel, "first", outs, ta, weights)
    qb, lb, sb, chip = call(second_kernel, "second", outs + [((SEQS, DH, DH), B16)], tb, weights, sa)
    chip, qa, la, sa, qb, lb, sb, spot = lax.optimization_barrier((chip, qa, la, sa, qb, lb, sb, spot))

    square = (DH, DH)
    by_chip = lax.all_to_all(chip, "seq", 0, 0, tiled=True, axis_index_groups=QUAD)
    (total,) = call(total_kernel, "total", [(square, B16)], by_chip)
    totals = lax.all_gather(total, "seq", axis=0, axis_index_groups=ACROSS)
    (parts,) = call(parts_kernel, "parts", [((4,) + square, B16)], spot, by_chip, totals)
    back = lax.all_to_all(parts, "seq", 0, 0, tiled=True, axis_index_groups=QUAD)
    (out,) = call(
        final_kernel, "final", [((SEQS, 2, BLOCK, DH), B16)],
        spot, qa, qb, la, lb, back, sa, sb, norm_gain.reshape(2, DH),
    )
    out = lax.all_to_all(out.reshape(8, BLOCK, DH), ("seq", "dp"), 0, 0, tiled=True, axis_index_groups=OWNERS)
    (joined,) = call(
        join_kernel, "join", [((BLOCK, 8 * DH), B16)], out, out_away=True, scratch=[pltpu.SemaphoreType.DMA((8,))]
    )
    return joined[None]


def solution(mesh):
    in_specs = (P("dp", "seq", None), P(None, "seq", ("heads", "dp")), P(("heads", "dp")))
    out_specs = P("dp", "seq", "heads")
    return jax.shard_map(body, mesh=mesh, in_specs=in_specs, out_specs=out_specs, check_vma=False)
```

```python
import jax
import jax.numpy as jnp
from jax import lax
from jax.experimental import pallas as pl
from jax.experimental.pallas import tpu as pltpu
from jax.sharding import PartitionSpec as P

DH = 128
SEQ = 32
BLOCK = 128
SEQS = 4
WSCALE = 2.0**19
F32 = jnp.float32
B16 = jnp.bfloat16
SIBLING = [(i, i ^ 1) for i in range(SEQ)]


def holder(z, head):
    return 2 * z + (head ^ ((z ^ (z >> 2)) & 1))


QUAD = [[holder(4 * a + b, h) for b in range(4)] for a in range(4) for h in range(2)]
def head_of(place):
    return (place ^ (place >> 1) ^ (place >> 3)) & 1


SAME_HEAD = [[holder(z, h) for z in range(16)] for h in range(2)]
ACROSS = [[holder(4 * a + b, h) for a in range(4)] for b in range(4) for h in range(2)]
OWNERS = [[holder(z, h) * 4 + y for y in range(4) for h in range(2)] for z in range(16)]
VMEM = pl.BlockSpec(memory_space=pltpu.VMEM)
SMEM = pl.BlockSpec(memory_space=pltpu.SMEM)
PARAMS = pltpu.CompilerParams(vmem_limit_bytes=24 * 1024 * 1024)


def silu_b(v):
    return (v * jax.nn.sigmoid(v)).astype(B16)


def rows(s):
    return slice(s * BLOCK, (s + 1) * BLOCK)


def outer(k, v):
    return lax.dot_general(k, v, (((0,), (0,)), ((), ())), preferred_element_type=F32)


def local(q, k, v):
    scores = lax.dot_general(q, k, (((1,), (1,)), ((), ())), preferred_element_type=F32)
    causal = lax.broadcasted_iota(jnp.int32, scores.shape, 0) >= lax.broadcasted_iota(jnp.int32, scores.shape, 1)
    return jnp.dot(jnp.where(causal, scores, 0.0).astype(B16), v, preferred_element_type=F32)


def block_work(out, q_ref, l_ref, s_ref):
    q, k, v = silu_b(out[:, :DH]), silu_b(out[:, DH : 2 * DH]), out[:, 2 * DH :].astype(B16)
    q_ref[...] = q
    for s in range(SEQS):
        r = rows(s)
        s_ref[s] = outer(k[r], v[r])
        l_ref[r] = local(q[r], k[r], v[r])


def first_kernel(t_ref, w_ref, q_ref, l_ref, s_ref):
    block_work(jnp.dot(t_ref[...], w_ref[...], preferred_element_type=F32), q_ref, l_ref, s_ref)


def second_kernel(t_ref, w_ref, sa_ref, q_ref, l_ref, s_ref, chip_ref):
    block_work(jnp.dot(t_ref[...], w_ref[...], preferred_element_type=F32), q_ref, l_ref, s_ref)
    for s in range(SEQS):
        chip_ref[s] = (sa_ref[s] + s_ref[s]).astype(B16)


def heads_kernel(spot_ref, w_ref, keep_ref, give_ref):
    mine = head_of(spot_ref[0]) == 0
    for j in range(3):
        low, high = w_ref[j, :, :DH], w_ref[j, :, DH:]
        keep_ref[:, j * DH : (j + 1) * DH] = jnp.where(mine, low, high)
        give_ref[:, j * DH : (j + 1) * DH] = jnp.where(mine, high, low)


def to_half(w):
    return (w.astype(F32) * WSCALE).astype(jnp.float16)


def total_kernel(r_ref, o_ref):
    o_ref[...] = (r_ref[0].astype(F32) + r_ref[1].astype(F32) + r_ref[2].astype(F32) + r_ref[3].astype(F32)).astype(B16)


def parts_kernel(spot_ref, r_ref, totals_ref, o_ref):
    quad = spot_ref[0] >> 3
    before = jnp.zeros((DH, DH), F32)
    for a in range(3):
        before = before + jnp.where(a < quad, totals_ref[a].astype(F32), 0.0)
    o_ref[0] = before.astype(B16)
    for j in range(3):
        before = before + r_ref[j].astype(F32)
        o_ref[j + 1] = before.astype(B16)


def copies_kernel(t_ref, o_ref, sem):
    copies = [pltpu.make_async_copy(t_ref, o_ref.at[s], sem.at[s]) for s in range(SEQS)]
    for c in copies:
        c.start()
    for c in copies:
        c.wait()


def join_kernel(i_ref, o_ref, sem):
    count = i_ref.shape[0]
    copies = [pltpu.make_async_copy(i_ref.at[j], o_ref.at[:, pl.ds(j * DH, DH)], sem.at[j]) for j in range(count)]
    for c in copies:
        c.start()
    for c in copies:
        c.wait()


def final_kernel(spot_ref, qa_ref, qb_ref, la_ref, lb_ref, before_ref, sa_ref, sb_ref, gain_ref, o_ref):
    core, head = spot_ref[0] & 1, head_of(spot_ref[0])
    gain = jnp.where(head == 0, gain_ref[0:1], gain_ref[1:2])

    def normed(q, l, p):
        attn = l + jnp.dot(q, p.astype(B16), preferred_element_type=F32)
        scale = lax.rsqrt(jnp.mean(attn * attn, axis=-1, keepdims=True) + 1e-06)
        return (attn * scale * gain).astype(B16)

    for s in range(SEQS):
        r = rows(s)
        before = before_ref[s].astype(F32)
        pa = jnp.where(core == 0, before, before + sb_ref[s])
        pb = jnp.where(core == 0, before + sa_ref[s], before)
        o_ref[s, head] = normed(qa_ref[r], la_ref[r], pa)
        o_ref[s, 1 - head] = normed(qb_ref[r], lb_ref[r], pb)


def call(kernel, name, outs, *args, away=(), out_away=False, scratch=(), params=True):
    anywhere = pl.BlockSpec(memory_space=pl.ANY)
    return pl.pallas_call(
        kernel,
        name=name,
        out_shape=[jax.ShapeDtypeStruct(s, d) for s, d in outs],
        in_specs=[SMEM if a.dtype == jnp.int32 else anywhere if i in away else VMEM for i, a in enumerate(args)],
        out_specs=[anywhere if out_away else VMEM for _ in outs],
        scratch_shapes=list(scratch),
        compiler_params=PARAMS if params else None,
    )(*args)


def body(tokens, proj_weights, norm_gain):
    place = lax.axis_index("seq")
    core = place & 1
    spot = place.reshape(1)
    own = ((proj_weights.shape[1], 3 * DH), B16)
    keep, give = call(heads_kernel, "heads", [own, own], spot, proj_weights)
    keep = to_half(keep)
    got = lax.ppermute(to_half(give), "seq", SIBLING)
    (copies,) = call(
        copies_kernel, "copies", [((SEQS,) + tokens.shape[1:], B16)], tokens[0], out_away=True, params=False,
        scratch=[pltpu.SemaphoreType.DMA((SEQS,))],
    )
    copies, got = lax.optimization_barrier((copies, got))
    mine_t = lax.all_to_all(copies, "dp", 0, 0, tiled=True)
    first = core == 0
    pair = jnp.concatenate([jnp.where(first, keep, got), jnp.where(first, got, keep)], axis=0)
    full = lax.all_gather(pair, "seq", axis=0, tiled=True, axis_index_groups=SAME_HEAD)
    mine_t, full = lax.optimization_barrier((mine_t, full))
    other_t = lax.ppermute(mine_t, "seq", SIBLING)
    weights = (full.astype(F32) * (1.0 / WSCALE)).astype(B16)
    n = SEQS * BLOCK
    ta, tb = mine_t.reshape(n, -1), other_t.reshape(n, -1)
    outs = [((n, DH), B16), ((n, DH), F32), ((SEQS, DH, DH), F32)]
    qa, la, sa = call(first_kernel, "first", outs, ta, weights)
    qb, lb, sb, chip = call(second_kernel, "second", outs + [((SEQS, DH, DH), B16)], tb, weights, sa)
    chip, qa, la, sa, qb, lb, sb, spot = lax.optimization_barrier((chip, qa, la, sa, qb, lb, sb, spot))

    square = (DH, DH)
    by_chip = lax.all_to_all(chip, "seq", 0, 0, tiled=True, axis_index_groups=QUAD)
    (total,) = call(total_kernel, "total", [(square, B16)], by_chip)
    totals = lax.all_gather(total, "seq", axis=0, axis_index_groups=ACROSS)
    (parts,) = call(parts_kernel, "parts", [((4,) + square, B16)], spot, by_chip, totals)
    back = lax.all_to_all(parts, "seq", 0, 0, tiled=True, axis_index_groups=QUAD)
    (out,) = call(
        final_kernel, "final", [((SEQS, 2, BLOCK, DH), B16)],
        spot, qa, qb, la, lb, back, sa, sb, norm_gain.reshape(2, DH),
    )
    out = lax.all_to_all(out.reshape(8, BLOCK, DH), ("seq", "dp"), 0, 0, tiled=True, axis_index_groups=OWNERS)
    (joined,) = call(
        join_kernel, "join", [((BLOCK, 8 * DH), B16)], out, out_away=True, scratch=[pltpu.SemaphoreType.DMA((8,))]
    )
    return joined[None]


def solution(mesh):
    in_specs = (P("dp", "seq", None), P(None, "seq", ("heads", "dp")), P(("heads", "dp")))
    out_specs = P("dp", "seq", "heads")
    return jax.shard_map(body, mesh=mesh, in_specs=in_specs, out_specs=out_specs, check_vma=False)
```

```python
import jax
import jax.numpy as jnp
from jax import lax
from jax.experimental import pallas as pl
from jax.experimental.pallas import tpu as pltpu
from jax.sharding import PartitionSpec as P

DH = 128
SEQ = 32
BLOCK = 128
SEQS = 4
WSCALE = 2.0**19
F32 = jnp.float32
B16 = jnp.bfloat16
SIBLING = [(i, i ^ 1) for i in range(SEQ)]


def holder(z, head):
    return 2 * z + (head ^ ((z ^ (z >> 2)) & 1))


QUAD = [[holder(4 * a + b, h) for b in range(4)] for a in range(4) for h in range(2)]
def head_of(place):
    return (place ^ (place >> 1) ^ (place >> 3)) & 1


SAME_HEAD = [[holder(z, h) for z in range(16)] for h in range(2)]
FORWARD = [[(holder(z, h), holder(z + d, h)) for z in range(16 - d) for h in range(2)] for d in (4, 8, 12)]
OWNERS = [[holder(z, h) * 4 + y for y in range(4) for h in range(2)] for z in range(16)]
VMEM = pl.BlockSpec(memory_space=pltpu.VMEM)
SMEM = pl.BlockSpec(memory_space=pltpu.SMEM)
PARAMS = pltpu.CompilerParams(vmem_limit_bytes=24 * 1024 * 1024)


def silu_b(v):
    return (v * jax.nn.sigmoid(v)).astype(B16)


def rows(s):
    return slice(s * BLOCK, (s + 1) * BLOCK)


def outer(k, v):
    return lax.dot_general(k, v, (((0,), (0,)), ((), ())), preferred_element_type=F32)


def local(q, k, v):
    scores = lax.dot_general(q, k, (((1,), (1,)), ((), ())), preferred_element_type=F32)
    causal = lax.broadcasted_iota(jnp.int32, scores.shape, 0) >= lax.broadcasted_iota(jnp.int32, scores.shape, 1)
    return jnp.dot(jnp.where(causal, scores, 0.0).astype(B16), v, preferred_element_type=F32)


def block_work(out, q_ref, l_ref, s_ref):
    q, k, v = silu_b(out[:, :DH]), silu_b(out[:, DH : 2 * DH]), out[:, 2 * DH :].astype(B16)
    q_ref[...] = q
    for s in range(SEQS):
        r = rows(s)
        s_ref[s] = outer(k[r], v[r])
        l_ref[r] = local(q[r], k[r], v[r])


def first_kernel(t_ref, w_ref, q_ref, l_ref, s_ref):
    block_work(jnp.dot(t_ref[...], w_ref[...], preferred_element_type=F32), q_ref, l_ref, s_ref)


def second_kernel(t_ref, w_ref, sa_ref, k_ref, v_ref, s_ref, chip_ref):
    kv = jnp.dot(t_ref[...], w_ref[:, DH:], preferred_element_type=F32)
    k, v = silu_b(kv[:, :DH]), kv[:, DH:].astype(B16)
    k_ref[...] = k
    v_ref[...] = v
    for s in range(SEQS):
        r = rows(s)
        state = outer(k[r], v[r])
        s_ref[s] = state
        chip_ref[s] = (sa_ref[s] + state).astype(B16)


def late_kernel(t_ref, w_ref, k_ref, v_ref, q_ref, l_ref):
    q = silu_b(jnp.dot(t_ref[...], w_ref[:, :DH], preferred_element_type=F32))
    q_ref[...] = q
    for s in range(SEQS):
        r = rows(s)
        l_ref[r] = local(q[r], k_ref[r], v_ref[r])


def heads_kernel(spot_ref, w_ref, keep_ref, give_ref):
    mine = head_of(spot_ref[0]) == 0
    for j in range(3):
        low, high = w_ref[j, :, :DH], w_ref[j, :, DH:]
        keep_ref[:, j * DH : (j + 1) * DH] = jnp.where(mine, low, high)
        give_ref[:, j * DH : (j + 1) * DH] = jnp.where(mine, high, low)


def to_half(w):
    return (w.astype(F32) * WSCALE).astype(jnp.float16)


def total_kernel(r_ref, o_ref):
    o_ref[...] = (r_ref[0].astype(F32) + r_ref[1].astype(F32) + r_ref[2].astype(F32) + r_ref[3].astype(F32)).astype(B16)


def parts_kernel(r_ref, one_ref, two_ref, three_ref, o_ref):
    before = one_ref[...].astype(F32) + two_ref[...].astype(F32) + three_ref[...].astype(F32)
    o_ref[0] = before.astype(B16)
    for j in range(3):
        before = before + r_ref[j].astype(F32)
        o_ref[j + 1] = before.astype(B16)


def copies_kernel(t_ref, o_ref, sem):
    copies = [pltpu.make_async_copy(t_ref, o_ref.at[s], sem.at[s]) for s in range(SEQS)]
    for c in copies:
        c.start()
    for c in copies:
        c.wait()


def join_kernel(i_ref, o_ref, sem):
    count = i_ref.shape[0]
    copies = [pltpu.make_async_copy(i_ref.at[j], o_ref.at[:, pl.ds(j * DH, DH)], sem.at[j]) for j in range(count)]
    for c in copies:
        c.start()
    for c in copies:
        c.wait()


def final_kernel(spot_ref, qa_ref, qb_ref, la_ref, lb_ref, before_ref, sa_ref, sb_ref, gain_ref, o_ref):
    core, head = spot_ref[0] & 1, head_of(spot_ref[0])
    gain = jnp.where(head == 0, gain_ref[0:1], gain_ref[1:2])

    def normed(q, l, p):
        attn = l + jnp.dot(q, p.astype(B16), preferred_element_type=F32)
        scale = lax.rsqrt(jnp.mean(attn * attn, axis=-1, keepdims=True) + 1e-06)
        return (attn * scale * gain).astype(B16)

    for s in range(SEQS):
        r = rows(s)
        before = before_ref[s].astype(F32)
        pa = jnp.where(core == 0, before, before + sb_ref[s])
        pb = jnp.where(core == 0, before + sa_ref[s], before)
        o_ref[s, head] = normed(qa_ref[r], la_ref[r], pa)
        o_ref[s, 1 - head] = normed(qb_ref[r], lb_ref[r], pb)


def call(kernel, name, outs, *args, away=(), out_away=False, scratch=(), params=True):
    anywhere = pl.BlockSpec(memory_space=pl.ANY)
    return pl.pallas_call(
        kernel,
        name=name,
        out_shape=[jax.ShapeDtypeStruct(s, d) for s, d in outs],
        in_specs=[SMEM if a.dtype == jnp.int32 else anywhere if i in away else VMEM for i, a in enumerate(args)],
        out_specs=[anywhere if out_away else VMEM for _ in outs],
        scratch_shapes=list(scratch),
        compiler_params=PARAMS if params else None,
    )(*args)


def body(tokens, proj_weights, norm_gain):
    place = lax.axis_index("seq")
    core = place & 1
    spot = place.reshape(1)
    own = ((proj_weights.shape[1], 3 * DH), B16)
    keep, give = call(heads_kernel, "heads", [own, own], spot, proj_weights)
    keep = to_half(keep)
    got = lax.ppermute(to_half(give), "seq", SIBLING)
    (copies,) = call(
        copies_kernel, "copies", [((SEQS,) + tokens.shape[1:], B16)], tokens[0], out_away=True, params=False,
        scratch=[pltpu.SemaphoreType.DMA((SEQS,))],
    )
    copies, got = lax.optimization_barrier((copies, got))
    mine_t = lax.all_to_all(copies, "dp", 0, 0, tiled=True)
    first = core == 0
    pair = jnp.concatenate([jnp.where(first, keep, got), jnp.where(first, got, keep)], axis=0)
    full = lax.all_gather(pair, "seq", axis=0, tiled=True, axis_index_groups=SAME_HEAD)
    weights = (full.astype(F32) * (1.0 / WSCALE)).astype(B16)
    mine_t, weights = lax.optimization_barrier((mine_t, weights))
    other_t = lax.ppermute(mine_t, "seq", SIBLING)
    n = SEQS * BLOCK
    ta, tb = mine_t.reshape(n, -1), other_t.reshape(n, -1)
    outs = [((n, DH), B16), ((n, DH), F32), ((SEQS, DH, DH), F32)]
    qa, la, sa = call(first_kernel, "first", outs, ta, weights)
    square = (DH, DH)
    kb, vb, sb, chip = call(
        second_kernel, "second", [((n, DH), B16), ((n, DH), B16), ((SEQS, DH, DH), F32), ((SEQS, DH, DH), B16)], tb, weights, sa
    )
    chip, qa, la, sa, kb, vb, sb, tb, weights, spot = lax.optimization_barrier((chip, qa, la, sa, kb, vb, sb, tb, weights, spot))
    by_chip = lax.all_to_all(chip, "seq", 0, 0, tiled=True, axis_index_groups=QUAD)
    by_chip, tb = lax.optimization_barrier((by_chip, tb))
    (total,) = call(total_kernel, "total", [(square, B16)], by_chip)
    earlier = [lax.ppermute(total, "seq", route) for route in FORWARD]
    qb, lb = call(late_kernel, "late", [((n, DH), B16), ((n, DH), F32)], tb, weights, kb, vb)
    earlier, qb, lb = lax.optimization_barrier((earlier, qb, lb))
    (parts,) = call(parts_kernel, "parts", [((4,) + square, B16)], by_chip, *earlier)
    back = lax.all_to_all(parts, "seq", 0, 0, tiled=True, axis_index_groups=QUAD)
    (out,) = call(
        final_kernel, "final", [((SEQS, 2, BLOCK, DH), B16)],
        spot, qa, qb, la, lb, back, sa, sb, norm_gain.reshape(2, DH),
    )
    out = lax.all_to_all(out.reshape(8, BLOCK, DH), ("seq", "dp"), 0, 0, tiled=True, axis_index_groups=OWNERS)
    (joined,) = call(
        join_kernel, "join", [((BLOCK, 8 * DH), B16)], out, out_away=True, scratch=[pltpu.SemaphoreType.DMA((8,))]
    )
    return joined[None]


def solution(mesh):
    in_specs = (P("dp", "seq", None), P(None, "seq", ("heads", "dp")), P(("heads", "dp")))
    out_specs = P("dp", "seq", "heads")
    return jax.shard_map(body, mesh=mesh, in_specs=in_specs, out_specs=out_specs, check_vma=False)
```

```python
import jax
import jax.numpy as jnp
from jax import lax
from jax.experimental import pallas as pl
from jax.experimental.pallas import tpu as pltpu
from jax.sharding import PartitionSpec as P

DH = 128
SEQ = 32
BLOCK = 128
SEQS = 4
WSCALE = 2.0**19
F32 = jnp.float32
B16 = jnp.bfloat16
SIBLING = [(i, i ^ 1) for i in range(SEQ)]


def holder(z, head):
    return 2 * z + (head ^ ((z ^ (z >> 2)) & 1))


QUAD = [[holder(4 * a + b, h) for b in range(4)] for a in range(4) for h in range(2)]
def head_of(place):
    return (place ^ (place >> 1) ^ (place >> 3)) & 1


SAME_HEAD = [[holder(z, h) for z in range(16)] for h in range(2)]
FORWARD = [[(holder(z, h), holder(z + d, h)) for z in range(16 - d) for h in range(2)] for d in (8, 12, 4)]
OWNERS = [[holder(z, h) * 4 + y for y in range(4) for h in range(2)] for z in range(16)]
VMEM = pl.BlockSpec(memory_space=pltpu.VMEM)
SMEM = pl.BlockSpec(memory_space=pltpu.SMEM)
PARAMS = pltpu.CompilerParams(vmem_limit_bytes=24 * 1024 * 1024)


def silu_b(v):
    return (v * jax.nn.sigmoid(v)).astype(B16)


def rows(s):
    return slice(s * BLOCK, (s + 1) * BLOCK)


def outer(k, v):
    return lax.dot_general(k, v, (((0,), (0,)), ((), ())), preferred_element_type=F32)


def local(q, k, v):
    scores = lax.dot_general(q, k, (((1,), (1,)), ((), ())), preferred_element_type=F32)
    causal = lax.broadcasted_iota(jnp.int32, scores.shape, 0) >= lax.broadcasted_iota(jnp.int32, scores.shape, 1)
    return jnp.dot(jnp.where(causal, scores, 0.0).astype(B16), v, preferred_element_type=F32)


def block_work(out, q_ref, l_ref, s_ref):
    q, k, v = silu_b(out[:, :DH]), silu_b(out[:, DH : 2 * DH]), out[:, 2 * DH :].astype(B16)
    q_ref[...] = q
    for s in range(SEQS):
        r = rows(s)
        s_ref[s] = outer(k[r], v[r])
        l_ref[r] = local(q[r], k[r], v[r])


def first_kernel(t_ref, w_ref, q_ref, l_ref, s_ref):
    block_work(jnp.dot(t_ref[...], w_ref[...], preferred_element_type=F32), q_ref, l_ref, s_ref)


def second_kernel(t_ref, w_ref, sa_ref, k_ref, v_ref, s_ref, chip_ref):
    kv = jnp.dot(t_ref[...], w_ref[:, DH:], preferred_element_type=F32)
    k, v = silu_b(kv[:, :DH]), kv[:, DH:].astype(B16)
    k_ref[...] = k
    v_ref[...] = v
    for s in range(SEQS):
        r = rows(s)
        state = outer(k[r], v[r])
        s_ref[s] = state
        chip_ref[s] = (sa_ref[s] + state).astype(B16)


def late_kernel(t_ref, w_ref, k_ref, v_ref, q_ref, l_ref):
    q = silu_b(jnp.dot(t_ref[...], w_ref[:, :DH], preferred_element_type=F32))
    q_ref[...] = q
    for s in range(SEQS):
        r = rows(s)
        l_ref[r] = local(q[r], k_ref[r], v_ref[r])


def heads_kernel(spot_ref, w_ref, keep_ref, give_ref):
    mine = head_of(spot_ref[0]) == 0
    for j in range(3):
        low, high = w_ref[j, :, :DH], w_ref[j, :, DH:]
        keep_ref[:, j * DH : (j + 1) * DH] = jnp.where(mine, low, high)
        give_ref[:, j * DH : (j + 1) * DH] = jnp.where(mine, high, low)


def to_half(w):
    return (w.astype(F32) * WSCALE).astype(jnp.float16)


def total_kernel(r_ref, o_ref):
    o_ref[...] = (r_ref[0].astype(F32) + r_ref[1].astype(F32) + r_ref[2].astype(F32) + r_ref[3].astype(F32)).astype(B16)


def parts_kernel(r_ref, one_ref, two_ref, three_ref, o_ref):
    before = one_ref[...].astype(F32) + two_ref[...].astype(F32) + three_ref[...].astype(F32)
    o_ref[0] = before.astype(B16)
    for j in range(3):
        before = before + r_ref[j].astype(F32)
        o_ref[j + 1] = before.astype(B16)


def copies_kernel(t_ref, o_ref, sem):
    copies = [pltpu.make_async_copy(t_ref, o_ref.at[s], sem.at[s]) for s in range(SEQS)]
    for c in copies:
        c.start()
    for c in copies:
        c.wait()


def join_kernel(i_ref, o_ref, sem):
    count = i_ref.shape[0]
    copies = [pltpu.make_async_copy(i_ref.at[j], o_ref.at[:, pl.ds(j * DH, DH)], sem.at[j]) for j in range(count)]
    for c in copies:
        c.start()
    for c in copies:
        c.wait()


def final_kernel(spot_ref, qa_ref, qb_ref, la_ref, lb_ref, before_ref, sa_ref, sb_ref, gain_ref, o_ref):
    core, head = spot_ref[0] & 1, head_of(spot_ref[0])
    gain = jnp.where(head == 0, gain_ref[0:1], gain_ref[1:2])

    def normed(q, l, p):
        attn = l + jnp.dot(q, p.astype(B16), preferred_element_type=F32)
        scale = lax.rsqrt(jnp.mean(attn * attn, axis=-1, keepdims=True) + 1e-06)
        return (attn * scale * gain).astype(B16)

    for s in range(SEQS):
        r = rows(s)
        before = before_ref[s].astype(F32)
        pa = jnp.where(core == 0, before, before + sb_ref[s])
        pb = jnp.where(core == 0, before + sa_ref[s], before)
        o_ref[s, head] = normed(qa_ref[r], la_ref[r], pa)
        o_ref[s, 1 - head] = normed(qb_ref[r], lb_ref[r], pb)


def call(kernel, name, outs, *args, away=(), out_away=False, scratch=(), params=True):
    anywhere = pl.BlockSpec(memory_space=pl.ANY)
    return pl.pallas_call(
        kernel,
        name=name,
        out_shape=[jax.ShapeDtypeStruct(s, d) for s, d in outs],
        in_specs=[SMEM if a.dtype == jnp.int32 else anywhere if i in away else VMEM for i, a in enumerate(args)],
        out_specs=[anywhere if out_away else VMEM for _ in outs],
        scratch_shapes=list(scratch),
        compiler_params=PARAMS if params else None,
    )(*args)


def body(tokens, proj_weights, norm_gain):
    place = lax.axis_index("seq")
    core = place & 1
    spot = place.reshape(1)
    own = ((proj_weights.shape[1], 3 * DH), B16)
    keep, give = call(heads_kernel, "heads", [own, own], spot, proj_weights)
    keep = to_half(keep)
    got = lax.ppermute(to_half(give), "seq", SIBLING)
    (copies,) = call(
        copies_kernel, "copies", [((SEQS,) + tokens.shape[1:], B16)], tokens[0], out_away=True, params=False,
        scratch=[pltpu.SemaphoreType.DMA((SEQS,))],
    )
    copies, got = lax.optimization_barrier((copies, got))
    mine_t = lax.all_to_all(copies, "dp", 0, 0, tiled=True)
    first = core == 0
    pair = jnp.concatenate([jnp.where(first, keep, got), jnp.where(first, got, keep)], axis=0)
    full = lax.all_gather(pair, "seq", axis=0, tiled=True, axis_index_groups=SAME_HEAD)
    weights = (full.astype(F32) * (1.0 / WSCALE)).astype(B16)
    mine_t, weights = lax.optimization_barrier((mine_t, weights))
    other_t = lax.ppermute(mine_t, "seq", SIBLING)
    n = SEQS * BLOCK
    ta, tb = mine_t.reshape(n, -1), other_t.reshape(n, -1)
    outs = [((n, DH), B16), ((n, DH), F32), ((SEQS, DH, DH), F32)]
    qa, la, sa = call(first_kernel, "first", outs, ta, weights)
    square = (DH, DH)
    kb, vb, sb, chip = call(
        second_kernel, "second", [((n, DH), B16), ((n, DH), B16), ((SEQS, DH, DH), F32), ((SEQS, DH, DH), B16)], tb, weights, sa
    )
    chip, qa, la, sa, kb, vb, sb, tb, weights, spot = lax.optimization_barrier((chip, qa, la, sa, kb, vb, sb, tb, weights, spot))
    by_chip = lax.all_to_all(chip, "seq", 0, 0, tiled=True, axis_index_groups=QUAD)
    by_chip, tb = lax.optimization_barrier((by_chip, tb))
    (total,) = call(total_kernel, "total", [(square, B16)], by_chip)
    earlier = [lax.ppermute(total, "seq", route) for route in FORWARD]
    qb, lb = call(late_kernel, "late", [((n, DH), B16), ((n, DH), F32)], tb, weights, kb, vb)
    earlier, qb, lb = lax.optimization_barrier((earlier, qb, lb))
    (parts,) = call(parts_kernel, "parts", [((4,) + square, B16)], by_chip, *earlier)
    back = lax.all_to_all(parts, "seq", 0, 0, tiled=True, axis_index_groups=QUAD)
    (out,) = call(
        final_kernel, "final", [((SEQS, 2, BLOCK, DH), B16)],
        spot, qa, qb, la, lb, back, sa, sb, norm_gain.reshape(2, DH),
    )
    out = lax.all_to_all(out.reshape(8, BLOCK, DH), ("seq", "dp"), 0, 0, tiled=True, axis_index_groups=OWNERS)
    (joined,) = call(
        join_kernel, "join", [((BLOCK, 8 * DH), B16)], out, out_away=True, scratch=[pltpu.SemaphoreType.DMA((8,))]
    )
    return joined[None]


def solution(mesh):
    in_specs = (P("dp", "seq", None), P(None, "seq", ("heads", "dp")), P(("heads", "dp")))
    out_specs = P("dp", "seq", "heads")
    return jax.shard_map(body, mesh=mesh, in_specs=in_specs, out_specs=out_specs, check_vma=False)
```

```python
import jax
import jax.numpy as jnp
from jax import lax
from jax.experimental import pallas as pl
from jax.experimental.pallas import tpu as pltpu
from jax.sharding import PartitionSpec as P

DH = 128
SEQ = 32
BLOCK = 128
SEQS = 4
WSCALE = 2.0**19
F32 = jnp.float32
B16 = jnp.bfloat16
SIBLING = [(i, i ^ 1) for i in range(SEQ)]


def holder(z, head):
    return 2 * z + (head ^ ((z ^ (z >> 2)) & 1))


QUAD = [[holder(4 * a + b, h) for b in range(4)] for a in range(4) for h in range(2)]
def head_of(place):
    return (place ^ (place >> 1) ^ (place >> 3)) & 1


SAME_HEAD = [[holder(z, h) for z in range(16)] for h in range(2)]
FORWARD = [[(holder(z, h), holder(z + d, h)) for z in range(16 - d) for h in range(2)] for d in (12, 8, 4)]
OWNERS = [[holder(z, h) * 4 + y for y in range(4) for h in range(2)] for z in range(16)]
VMEM = pl.BlockSpec(memory_space=pltpu.VMEM)
SMEM = pl.BlockSpec(memory_space=pltpu.SMEM)
PARAMS = pltpu.CompilerParams(vmem_limit_bytes=24 * 1024 * 1024)


def silu_b(v):
    return (v * jax.nn.sigmoid(v)).astype(B16)


def rows(s):
    return slice(s * BLOCK, (s + 1) * BLOCK)


def outer(k, v):
    return lax.dot_general(k, v, (((0,), (0,)), ((), ())), preferred_element_type=F32)


def local(q, k, v):
    scores = lax.dot_general(q, k, (((1,), (1,)), ((), ())), preferred_element_type=F32)
    causal = lax.broadcasted_iota(jnp.int32, scores.shape, 0) >= lax.broadcasted_iota(jnp.int32, scores.shape, 1)
    return jnp.dot(jnp.where(causal, scores, 0.0).astype(B16), v, preferred_element_type=F32)


def block_work(out, q_ref, l_ref, s_ref):
    q, k, v = silu_b(out[:, :DH]), silu_b(out[:, DH : 2 * DH]), out[:, 2 * DH :].astype(B16)
    q_ref[...] = q
    for s in range(SEQS):
        r = rows(s)
        s_ref[s] = outer(k[r], v[r])
        l_ref[r] = local(q[r], k[r], v[r])


def first_kernel(t_ref, w_ref, q_ref, l_ref, s_ref):
    block_work(jnp.dot(t_ref[...], w_ref[...], preferred_element_type=F32), q_ref, l_ref, s_ref)


def second_kernel(t_ref, w_ref, sa_ref, k_ref, v_ref, s_ref, chip_ref):
    kv = jnp.dot(t_ref[...], w_ref[:, DH:], preferred_element_type=F32)
    k, v = silu_b(kv[:, :DH]), kv[:, DH:].astype(B16)
    k_ref[...] = k
    v_ref[...] = v
    for s in range(SEQS):
        r = rows(s)
        state = outer(k[r], v[r])
        s_ref[s] = state
        chip_ref[s] = (sa_ref[s] + state).astype(B16)


def late_kernel(t_ref, w_ref, k_ref, v_ref, q_ref, l_ref):
    q = silu_b(jnp.dot(t_ref[...], w_ref[:, :DH], preferred_element_type=F32))
    q_ref[...] = q
    for s in range(SEQS):
        r = rows(s)
        l_ref[r] = local(q[r], k_ref[r], v_ref[r])


def heads_kernel(spot_ref, w_ref, keep_ref, give_ref):
    mine = head_of(spot_ref[0]) == 0
    for j in range(3):
        low, high = w_ref[j, :, :DH], w_ref[j, :, DH:]
        keep_ref[:, j * DH : (j + 1) * DH] = jnp.where(mine, low, high)
        give_ref[:, j * DH : (j + 1) * DH] = jnp.where(mine, high, low)


def to_half(w):
    return (w.astype(F32) * WSCALE).astype(jnp.float16)


def total_kernel(r_ref, o_ref):
    o_ref[...] = (r_ref[0].astype(F32) + r_ref[1].astype(F32) + r_ref[2].astype(F32) + r_ref[3].astype(F32)).astype(B16)


def parts_kernel(r_ref, one_ref, two_ref, three_ref, o_ref):
    before = one_ref[...].astype(F32) + two_ref[...].astype(F32) + three_ref[...].astype(F32)
    o_ref[0] = before.astype(B16)
    for j in range(3):
        before = before + r_ref[j].astype(F32)
        o_ref[j + 1] = before.astype(B16)


def copies_kernel(t_ref, o_ref, sem):
    copies = [pltpu.make_async_copy(t_ref, o_ref.at[s], sem.at[s]) for s in range(SEQS)]
    for c in copies:
        c.start()
    for c in copies:
        c.wait()


def join_kernel(i_ref, o_ref, sem):
    count = i_ref.shape[0]
    copies = [pltpu.make_async_copy(i_ref.at[j], o_ref.at[:, pl.ds(j * DH, DH)], sem.at[j]) for j in range(count)]
    for c in copies:
        c.start()
    for c in copies:
        c.wait()


def final_kernel(spot_ref, qa_ref, qb_ref, la_ref, lb_ref, before_ref, sa_ref, sb_ref, gain_ref, o_ref):
    core, head = spot_ref[0] & 1, head_of(spot_ref[0])
    gain = jnp.where(head == 0, gain_ref[0:1], gain_ref[1:2])

    def normed(q, l, p):
        attn = l + jnp.dot(q, p.astype(B16), preferred_element_type=F32)
        scale = lax.rsqrt(jnp.mean(attn * attn, axis=-1, keepdims=True) + 1e-06)
        return (attn * scale * gain).astype(B16)

    for s in range(SEQS):
        r = rows(s)
        before = before_ref[s].astype(F32)
        pa = jnp.where(core == 0, before, before + sb_ref[s])
        pb = jnp.where(core == 0, before + sa_ref[s], before)
        o_ref[s, head] = normed(qa_ref[r], la_ref[r], pa)
        o_ref[s, 1 - head] = normed(qb_ref[r], lb_ref[r], pb)


def call(kernel, name, outs, *args, away=(), out_away=False, scratch=(), params=True):
    anywhere = pl.BlockSpec(memory_space=pl.ANY)
    return pl.pallas_call(
        kernel,
        name=name,
        out_shape=[jax.ShapeDtypeStruct(s, d) for s, d in outs],
        in_specs=[SMEM if a.dtype == jnp.int32 else anywhere if i in away else VMEM for i, a in enumerate(args)],
        out_specs=[anywhere if out_away else VMEM for _ in outs],
        scratch_shapes=list(scratch),
        compiler_params=PARAMS if params else None,
    )(*args)


def body(tokens, proj_weights, norm_gain):
    place = lax.axis_index("seq")
    core = place & 1
    spot = place.reshape(1)
    own = ((proj_weights.shape[1], 3 * DH), B16)
    keep, give = call(heads_kernel, "heads", [own, own], spot, proj_weights)
    keep = to_half(keep)
    got = lax.ppermute(to_half(give), "seq", SIBLING)
    (copies,) = call(
        copies_kernel, "copies", [((SEQS,) + tokens.shape[1:], B16)], tokens[0], out_away=True, params=False,
        scratch=[pltpu.SemaphoreType.DMA((SEQS,))],
    )
    copies, got = lax.optimization_barrier((copies, got))
    mine_t = lax.all_to_all(copies, "dp", 0, 0, tiled=True)
    first = core == 0
    pair = jnp.concatenate([jnp.where(first, keep, got), jnp.where(first, got, keep)], axis=0)
    full = lax.all_gather(pair, "seq", axis=0, tiled=True, axis_index_groups=SAME_HEAD)
    weights = (full.astype(F32) * (1.0 / WSCALE)).astype(B16)
    mine_t, weights = lax.optimization_barrier((mine_t, weights))
    other_t = lax.ppermute(mine_t, "seq", SIBLING)
    n = SEQS * BLOCK
    ta, tb = mine_t.reshape(n, -1), other_t.reshape(n, -1)
    outs = [((n, DH), B16), ((n, DH), F32), ((SEQS, DH, DH), F32)]
    qa, la, sa = call(first_kernel, "first", outs, ta, weights)
    square = (DH, DH)
    kb, vb, sb, chip = call(
        second_kernel, "second", [((n, DH), B16), ((n, DH), B16), ((SEQS, DH, DH), F32), ((SEQS, DH, DH), B16)], tb, weights, sa
    )
    chip, qa, la, sa, kb, vb, sb, tb, weights, spot = lax.optimization_barrier((chip, qa, la, sa, kb, vb, sb, tb, weights, spot))
    by_chip = lax.all_to_all(chip, "seq", 0, 0, tiled=True, axis_index_groups=QUAD)
    by_chip, tb = lax.optimization_barrier((by_chip, tb))
    (total,) = call(total_kernel, "total", [(square, B16)], by_chip)
    earlier = [lax.ppermute(total, "seq", route) for route in FORWARD]
    qb, lb = call(late_kernel, "late", [((n, DH), B16), ((n, DH), F32)], tb, weights, kb, vb)
    earlier, qb, lb = lax.optimization_barrier((earlier, qb, lb))
    (parts,) = call(parts_kernel, "parts", [((4,) + square, B16)], by_chip, *earlier)
    back = lax.all_to_all(parts, "seq", 0, 0, tiled=True, axis_index_groups=QUAD)
    (out,) = call(
        final_kernel, "final", [((SEQS, 2, BLOCK, DH), B16)],
        spot, qa, qb, la, lb, back, sa, sb, norm_gain.reshape(2, DH),
    )
    out = lax.all_to_all(out.reshape(8, BLOCK, DH), ("seq", "dp"), 0, 0, tiled=True, axis_index_groups=OWNERS)
    (joined,) = call(
        join_kernel, "join", [((BLOCK, 8 * DH), B16)], out, out_away=True, scratch=[pltpu.SemaphoreType.DMA((8,))]
    )
    return joined[None]


def solution(mesh):
    in_specs = (P("dp", "seq", None), P(None, "seq", ("heads", "dp")), P(("heads", "dp")))
    out_specs = P("dp", "seq", "heads")
    return jax.shard_map(body, mesh=mesh, in_specs=in_specs, out_specs=out_specs, check_vma=False)
```

```python
import jax
import jax.numpy as jnp
from jax import lax
from jax.experimental import pallas as pl
from jax.experimental.pallas import tpu as pltpu
from jax.sharding import PartitionSpec as P

DH = 128
SEQ = 32
BLOCK = 128
SEQS = 4
WSCALE = 2.0**19
F32 = jnp.float32
B16 = jnp.bfloat16
SIBLING = [(i, i ^ 1) for i in range(SEQ)]


def holder(z, head):
    return 2 * z + (head ^ ((z ^ (z >> 2)) & 1))


QUAD = [[holder(4 * a + b, h) for b in range(4)] for a in range(4) for h in range(2)]
def head_of(place):
    return (place ^ (place >> 1) ^ (place >> 3)) & 1


SAME_HEAD = [[holder(z, h) for z in range(16)] for h in range(2)]
FORWARD = [[(holder(z, h), holder(z + d, h)) for z in range(16 - d) for h in range(2)] for d in (8, 4, 12)]
OWNERS = [[holder(z, h) * 4 + y for y in range(4) for h in range(2)] for z in range(16)]
VMEM = pl.BlockSpec(memory_space=pltpu.VMEM)
SMEM = pl.BlockSpec(memory_space=pltpu.SMEM)
PARAMS = pltpu.CompilerParams(vmem_limit_bytes=24 * 1024 * 1024)


def silu_b(v):
    return (v * jax.nn.sigmoid(v)).astype(B16)


def rows(s):
    return slice(s * BLOCK, (s + 1) * BLOCK)


def outer(k, v):
    return lax.dot_general(k, v, (((0,), (0,)), ((), ())), preferred_element_type=F32)


def local(q, k, v):
    scores = lax.dot_general(q, k, (((1,), (1,)), ((), ())), preferred_element_type=F32)
    causal = lax.broadcasted_iota(jnp.int32, scores.shape, 0) >= lax.broadcasted_iota(jnp.int32, scores.shape, 1)
    return jnp.dot(jnp.where(causal, scores, 0.0).astype(B16), v, preferred_element_type=F32)


def block_work(out, q_ref, l_ref, s_ref):
    q, k, v = silu_b(out[:, :DH]), silu_b(out[:, DH : 2 * DH]), out[:, 2 * DH :].astype(B16)
    q_ref[...] = q
    for s in range(SEQS):
        r = rows(s)
        s_ref[s] = outer(k[r], v[r])
        l_ref[r] = local(q[r], k[r], v[r])


def first_kernel(t_ref, w_ref, q_ref, l_ref, s_ref):
    block_work(jnp.dot(t_ref[...], w_ref[...], preferred_element_type=F32), q_ref, l_ref, s_ref)


def second_kernel(t_ref, w_ref, sa_ref, k_ref, v_ref, s_ref, chip_ref):
    kv = jnp.dot(t_ref[...], w_ref[:, DH:], preferred_element_type=F32)
    k, v = silu_b(kv[:, :DH]), kv[:, DH:].astype(B16)
    k_ref[...] = k
    v_ref[...] = v
    for s in range(SEQS):
        r = rows(s)
        state = outer(k[r], v[r])
        s_ref[s] = state
        chip_ref[s] = (sa_ref[s] + state).astype(B16)


def late_kernel(t_ref, w_ref, k_ref, v_ref, q_ref, l_ref):
    q = silu_b(jnp.dot(t_ref[...], w_ref[:, :DH], preferred_element_type=F32))
    q_ref[...] = q
    for s in range(SEQS):
        r = rows(s)
        l_ref[r] = local(q[r], k_ref[r], v_ref[r])


def heads_kernel(spot_ref, w_ref, keep_ref, give_ref):
    mine = head_of(spot_ref[0]) == 0
    for j in range(3):
        low, high = w_ref[j, :, :DH], w_ref[j, :, DH:]
        keep_ref[:, j * DH : (j + 1) * DH] = jnp.where(mine, low, high)
        give_ref[:, j * DH : (j + 1) * DH] = jnp.where(mine, high, low)


def to_half(w):
    return (w.astype(F32) * WSCALE).astype(jnp.float16)


def total_kernel(r_ref, o_ref):
    o_ref[...] = (r_ref[0].astype(F32) + r_ref[1].astype(F32) + r_ref[2].astype(F32) + r_ref[3].astype(F32)).astype(B16)


def parts_kernel(r_ref, one_ref, two_ref, three_ref, o_ref):
    before = one_ref[...].astype(F32) + two_ref[...].astype(F32) + three_ref[...].astype(F32)
    o_ref[0] = before.astype(B16)
    for j in range(3):
        before = before + r_ref[j].astype(F32)
        o_ref[j + 1] = before.astype(B16)


def copies_kernel(t_ref, o_ref, sem):
    copies = [pltpu.make_async_copy(t_ref, o_ref.at[s], sem.at[s]) for s in range(SEQS)]
    for c in copies:
        c.start()
    for c in copies:
        c.wait()


def join_kernel(i_ref, o_ref, sem):
    count = i_ref.shape[0]
    copies = [pltpu.make_async_copy(i_ref.at[j], o_ref.at[:, pl.ds(j * DH, DH)], sem.at[j]) for j in range(count)]
    for c in copies:
        c.start()
    for c in copies:
        c.wait()


def final_kernel(spot_ref, qa_ref, qb_ref, la_ref, lb_ref, before_ref, sa_ref, sb_ref, gain_ref, o_ref):
    core, head = spot_ref[0] & 1, head_of(spot_ref[0])
    gain = jnp.where(head == 0, gain_ref[0:1], gain_ref[1:2])

    def normed(q, l, p):
        attn = l + jnp.dot(q, p.astype(B16), preferred_element_type=F32)
        scale = lax.rsqrt(jnp.mean(attn * attn, axis=-1, keepdims=True) + 1e-06)
        return (attn * scale * gain).astype(B16)

    for s in range(SEQS):
        r = rows(s)
        before = before_ref[s].astype(F32)
        pa = jnp.where(core == 0, before, before + sb_ref[s])
        pb = jnp.where(core == 0, before + sa_ref[s], before)
        o_ref[s, head] = normed(qa_ref[r], la_ref[r], pa)
        o_ref[s, 1 - head] = normed(qb_ref[r], lb_ref[r], pb)


def call(kernel, name, outs, *args, away=(), out_away=False, scratch=(), params=True):
    anywhere = pl.BlockSpec(memory_space=pl.ANY)
    return pl.pallas_call(
        kernel,
        name=name,
        out_shape=[jax.ShapeDtypeStruct(s, d) for s, d in outs],
        in_specs=[SMEM if a.dtype == jnp.int32 else anywhere if i in away else VMEM for i, a in enumerate(args)],
        out_specs=[anywhere if out_away else VMEM for _ in outs],
        scratch_shapes=list(scratch),
        compiler_params=PARAMS if params else None,
    )(*args)


def body(tokens, proj_weights, norm_gain):
    place = lax.axis_index("seq")
    core = place & 1
    spot = place.reshape(1)
    own = ((proj_weights.shape[1], 3 * DH), B16)
    keep, give = call(heads_kernel, "heads", [own, own], spot, proj_weights)
    keep = to_half(keep)
    got = lax.ppermute(to_half(give), "seq", SIBLING)
    (copies,) = call(
        copies_kernel, "copies", [((SEQS,) + tokens.shape[1:], B16)], tokens[0], out_away=True, params=False,
        scratch=[pltpu.SemaphoreType.DMA((SEQS,))],
    )
    copies, got = lax.optimization_barrier((copies, got))
    mine_t = lax.all_to_all(copies, "dp", 0, 0, tiled=True)
    first = core == 0
    pair = jnp.concatenate([jnp.where(first, keep, got), jnp.where(first, got, keep)], axis=0)
    full = lax.all_gather(pair, "seq", axis=0, tiled=True, axis_index_groups=SAME_HEAD)
    weights = (full.astype(F32) * (1.0 / WSCALE)).astype(B16)
    mine_t, weights = lax.optimization_barrier((mine_t, weights))
    other_t = lax.ppermute(mine_t, "seq", SIBLING)
    n = SEQS * BLOCK
    ta, tb = mine_t.reshape(n, -1), other_t.reshape(n, -1)
    outs = [((n, DH), B16), ((n, DH), F32), ((SEQS, DH, DH), F32)]
    qa, la, sa = call(first_kernel, "first", outs, ta, weights)
    square = (DH, DH)
    kb, vb, sb, chip = call(
        second_kernel, "second", [((n, DH), B16), ((n, DH), B16), ((SEQS, DH, DH), F32), ((SEQS, DH, DH), B16)], tb, weights, sa
    )
    chip, qa, la, sa, kb, vb, sb, tb, weights, spot = lax.optimization_barrier((chip, qa, la, sa, kb, vb, sb, tb, weights, spot))
    by_chip = lax.all_to_all(chip, "seq", 0, 0, tiled=True, axis_index_groups=QUAD)
    by_chip, tb = lax.optimization_barrier((by_chip, tb))
    (total,) = call(total_kernel, "total", [(square, B16)], by_chip)
    earlier = [lax.ppermute(total, "seq", route) for route in FORWARD]
    qb, lb = call(late_kernel, "late", [((n, DH), B16), ((n, DH), F32)], tb, weights, kb, vb)
    earlier, qb, lb = lax.optimization_barrier((earlier, qb, lb))
    (parts,) = call(parts_kernel, "parts", [((4,) + square, B16)], by_chip, *earlier)
    back = lax.all_to_all(parts, "seq", 0, 0, tiled=True, axis_index_groups=QUAD)
    (out,) = call(
        final_kernel, "final", [((SEQS, 2, BLOCK, DH), B16)],
        spot, qa, qb, la, lb, back, sa, sb, norm_gain.reshape(2, DH),
    )
    out = lax.all_to_all(out.reshape(8, BLOCK, DH), ("seq", "dp"), 0, 0, tiled=True, axis_index_groups=OWNERS)
    (joined,) = call(
        join_kernel, "join", [((BLOCK, 8 * DH), B16)], out, out_away=True, scratch=[pltpu.SemaphoreType.DMA((8,))]
    )
    return joined[None]


def solution(mesh):
    in_specs = (P("dp", "seq", None), P(None, "seq", ("heads", "dp")), P(("heads", "dp")))
    out_specs = P("dp", "seq", "heads")
    return jax.shard_map(body, mesh=mesh, in_specs=in_specs, out_specs=out_specs, check_vma=False)
```

```python
import jax
import jax.numpy as jnp
from jax import lax
from jax.experimental import pallas as pl
from jax.experimental.pallas import tpu as pltpu
from jax.sharding import PartitionSpec as P

DH = 128
SEQ = 32
BLOCK = 128
SEQS = 4
WSCALE = 2.0**19
F32 = jnp.float32
B16 = jnp.bfloat16
SIBLING = [(i, i ^ 1) for i in range(SEQ)]


def holder(z, head):
    return 2 * z + head


QUAD = [[holder(4 * a + b, h) for b in range(4)] for a in range(4) for h in range(2)]
def head_of(place):
    return place & 1


SAME_HEAD = [[holder(z, h) for z in range(16)] for h in range(2)]
FORWARD = [[(holder(z, h), holder(z + d, h)) for z in range(16 - d) for h in range(2)] for d in (8, 12, 4)]
OWNERS = [[holder(z, h) * 4 + y for y in range(4) for h in range(2)] for z in range(16)]
VMEM = pl.BlockSpec(memory_space=pltpu.VMEM)
SMEM = pl.BlockSpec(memory_space=pltpu.SMEM)
PARAMS = pltpu.CompilerParams(vmem_limit_bytes=24 * 1024 * 1024)


def silu_b(v):
    return (v * jax.nn.sigmoid(v)).astype(B16)


def rows(s):
    return slice(s * BLOCK, (s + 1) * BLOCK)


def outer(k, v):
    return lax.dot_general(k, v, (((0,), (0,)), ((), ())), preferred_element_type=F32)


def local(q, k, v):
    scores = lax.dot_general(q, k, (((1,), (1,)), ((), ())), preferred_element_type=F32)
    causal = lax.broadcasted_iota(jnp.int32, scores.shape, 0) >= lax.broadcasted_iota(jnp.int32, scores.shape, 1)
    return jnp.dot(jnp.where(causal, scores, 0.0).astype(B16), v, preferred_element_type=F32)


def block_work(out, q_ref, l_ref, s_ref):
    q, k, v = silu_b(out[:, :DH]), silu_b(out[:, DH : 2 * DH]), out[:, 2 * DH :].astype(B16)
    q_ref[...] = q
    for s in range(SEQS):
        r = rows(s)
        s_ref[s] = outer(k[r], v[r])
        l_ref[r] = local(q[r], k[r], v[r])


def first_kernel(t_ref, w_ref, q_ref, l_ref, s_ref):
    block_work(jnp.dot(t_ref[...], w_ref[...], preferred_element_type=F32), q_ref, l_ref, s_ref)


def second_kernel(t_ref, w_ref, sa_ref, k_ref, v_ref, s_ref, chip_ref):
    kv = jnp.dot(t_ref[...], w_ref[:, DH:], preferred_element_type=F32)
    k, v = silu_b(kv[:, :DH]), kv[:, DH:].astype(B16)
    k_ref[...] = k
    v_ref[...] = v
    for s in range(SEQS):
        r = rows(s)
        state = outer(k[r], v[r])
        s_ref[s] = state
        chip_ref[s] = (sa_ref[s] + state).astype(B16)


def late_kernel(t_ref, w_ref, k_ref, v_ref, q_ref, l_ref):
    q = silu_b(jnp.dot(t_ref[...], w_ref[:, :DH], preferred_element_type=F32))
    q_ref[...] = q
    for s in range(SEQS):
        r = rows(s)
        l_ref[r] = local(q[r], k_ref[r], v_ref[r])


def heads_kernel(spot_ref, w_ref, keep_ref, give_ref):
    mine = head_of(spot_ref[0]) == 0
    for j in range(3):
        low, high = w_ref[j, :, :DH], w_ref[j, :, DH:]
        keep_ref[:, j * DH : (j + 1) * DH] = jnp.where(mine, low, high)
        give_ref[:, j * DH : (j + 1) * DH] = jnp.where(mine, high, low)


def to_half(w):
    return (w.astype(F32) * WSCALE).astype(jnp.float16)


def total_kernel(r_ref, o_ref):
    o_ref[...] = (r_ref[0].astype(F32) + r_ref[1].astype(F32) + r_ref[2].astype(F32) + r_ref[3].astype(F32)).astype(B16)


def parts_kernel(r_ref, one_ref, two_ref, three_ref, o_ref):
    before = one_ref[...].astype(F32) + two_ref[...].astype(F32) + three_ref[...].astype(F32)
    o_ref[0] = before.astype(B16)
    for j in range(3):
        before = before + r_ref[j].astype(F32)
        o_ref[j + 1] = before.astype(B16)


def copies_kernel(t_ref, o_ref, sem):
    copies = [pltpu.make_async_copy(t_ref, o_ref.at[s], sem.at[s]) for s in range(SEQS)]
    for c in copies:
        c.start()
    for c in copies:
        c.wait()


def join_kernel(i_ref, o_ref, sem):
    count = i_ref.shape[0]
    copies = [pltpu.make_async_copy(i_ref.at[j], o_ref.at[:, pl.ds(j * DH, DH)], sem.at[j]) for j in range(count)]
    for c in copies:
        c.start()
    for c in copies:
        c.wait()


def final_kernel(spot_ref, qa_ref, qb_ref, la_ref, lb_ref, before_ref, sa_ref, sb_ref, gain_ref, o_ref):
    core, head = spot_ref[0] & 1, head_of(spot_ref[0])
    gain = jnp.where(head == 0, gain_ref[0:1], gain_ref[1:2])

    def normed(q, l, p):
        attn = l + jnp.dot(q, p.astype(B16), preferred_element_type=F32)
        scale = lax.rsqrt(jnp.mean(attn * attn, axis=-1, keepdims=True) + 1e-06)
        return (attn * scale * gain).astype(B16)

    for s in range(SEQS):
        r = rows(s)
        before = before_ref[s].astype(F32)
        pa = jnp.where(core == 0, before, before + sb_ref[s])
        pb = jnp.where(core == 0, before + sa_ref[s], before)
        o_ref[s, head] = normed(qa_ref[r], la_ref[r], pa)
        o_ref[s, 1 - head] = normed(qb_ref[r], lb_ref[r], pb)


def call(kernel, name, outs, *args, away=(), out_away=False, scratch=(), params=True):
    anywhere = pl.BlockSpec(memory_space=pl.ANY)
    return pl.pallas_call(
        kernel,
        name=name,
        out_shape=[jax.ShapeDtypeStruct(s, d) for s, d in outs],
        in_specs=[SMEM if a.dtype == jnp.int32 else anywhere if i in away else VMEM for i, a in enumerate(args)],
        out_specs=[anywhere if out_away else VMEM for _ in outs],
        scratch_shapes=list(scratch),
        compiler_params=PARAMS if params else None,
    )(*args)


def body(tokens, proj_weights, norm_gain):
    place = lax.axis_index("seq")
    core = place & 1
    spot = place.reshape(1)
    own = ((proj_weights.shape[1], 3 * DH), B16)
    keep, give = call(heads_kernel, "heads", [own, own], spot, proj_weights)
    keep = to_half(keep)
    got = lax.ppermute(to_half(give), "seq", SIBLING)
    (copies,) = call(
        copies_kernel, "copies", [((SEQS,) + tokens.shape[1:], B16)], tokens[0], out_away=True, params=False,
        scratch=[pltpu.SemaphoreType.DMA((SEQS,))],
    )
    copies, got = lax.optimization_barrier((copies, got))
    mine_t = lax.all_to_all(copies, "dp", 0, 0, tiled=True)
    first = core == 0
    pair = jnp.concatenate([jnp.where(first, keep, got), jnp.where(first, got, keep)], axis=0)
    full = lax.all_gather(pair, "seq", axis=0, tiled=True, axis_index_groups=SAME_HEAD)
    weights = (full.astype(F32) * (1.0 / WSCALE)).astype(B16)
    mine_t, weights = lax.optimization_barrier((mine_t, weights))
    other_t = lax.ppermute(mine_t, "seq", SIBLING)
    n = SEQS * BLOCK
    ta, tb = mine_t.reshape(n, -1), other_t.reshape(n, -1)
    outs = [((n, DH), B16), ((n, DH), F32), ((SEQS, DH, DH), F32)]
    qa, la, sa = call(first_kernel, "first", outs, ta, weights)
    square = (DH, DH)
    kb, vb, sb, chip = call(
        second_kernel, "second", [((n, DH), B16), ((n, DH), B16), ((SEQS, DH, DH), F32), ((SEQS, DH, DH), B16)], tb, weights, sa
    )
    chip, qa, la, sa, kb, vb, sb, tb, weights, spot = lax.optimization_barrier((chip, qa, la, sa, kb, vb, sb, tb, weights, spot))
    by_chip = lax.all_to_all(chip, "seq", 0, 0, tiled=True, axis_index_groups=QUAD)
    by_chip, tb = lax.optimization_barrier((by_chip, tb))
    (total,) = call(total_kernel, "total", [(square, B16)], by_chip)
    earlier = [lax.ppermute(total, "seq", route) for route in FORWARD]
    qb, lb = call(late_kernel, "late", [((n, DH), B16), ((n, DH), F32)], tb, weights, kb, vb)
    earlier, qb, lb = lax.optimization_barrier((earlier, qb, lb))
    (parts,) = call(parts_kernel, "parts", [((4,) + square, B16)], by_chip, *earlier)
    back = lax.all_to_all(parts, "seq", 0, 0, tiled=True, axis_index_groups=QUAD)
    (out,) = call(
        final_kernel, "final", [((SEQS, 2, BLOCK, DH), B16)],
        spot, qa, qb, la, lb, back, sa, sb, norm_gain.reshape(2, DH),
    )
    out = lax.all_to_all(out.reshape(8, BLOCK, DH), ("seq", "dp"), 0, 0, tiled=True, axis_index_groups=OWNERS)
    (joined,) = call(
        join_kernel, "join", [((BLOCK, 8 * DH), B16)], out, out_away=True, scratch=[pltpu.SemaphoreType.DMA((8,))]
    )
    return joined[None]


def solution(mesh):
    in_specs = (P("dp", "seq", None), P(None, "seq", ("heads", "dp")), P(("heads", "dp")))
    out_specs = P("dp", "seq", "heads")
    return jax.shard_map(body, mesh=mesh, in_specs=in_specs, out_specs=out_specs, check_vma=False)
```
